32 devices in a mesh: grp: 2 (over y), frame: 4 (over x, core), band: 4 (over z).
Axes of the slice: x: 2, y: 2, z: 4, core: 2. Of those that a mesh axis runs over, the one named last changes fastest.
Arguments:
- features: bfloat16 [16, 64, 128, 256], P(('grp', 'frame'), 'band'), parts along dimension 0, may hold values from -6 to 6
- space_kernel: bfloat16 [3, 3, 256, 256], replicated, may hold values from -0.125 to 0.125
- space_gain: float32 [256], replicated, may hold values from 0.5 to 2
- space_bias: float32 [256], replicated, may hold values from -3 to 3
- time_kernel: bfloat16 [3, 256, 256], replicated, may hold values from -0.21875 to 0.21875
- time_gain: float32 [256], replicated, may hold values from 0.5 to 2
- time_bias: float32 [256], replicated, may hold values from -3 to 3
Outputs:
- decoded: bfloat16 [16, 64, 128, 256], P(('grp', 'frame'), 'band'), parts along dimension 0
The draws below stay inside these ranges and needn't reach their ends.
There are 2 independent parts, one for each index of `grp`. The reference program is written for one: setup_inputs(seed, part) draws one part's arguments, and reference() takes and returns one part's arrays. A program takes and returns all parts, laid end to end along the dimension named above; an argument that names none is the same for every part. Nothing has to cross between parts.
All inputs are finite; a program needn't handle non-finite values.
Results may differ from the reference program's by a relative error of at most 0.0056.
Values may be sent and summed in bfloat16 or wider, within the bound.
A program may use at most 64 MiB of HBM per device.

```python
import math
import jax
import jax.numpy as jnp
from jax import lax

C = 256
W = 128
F = 8
H = 64


def block_scale(rng, shape, split, low, high):
    factor_of, own = 1.0, jax.random.fold_in(rng, 6)
    for dim, shards_of in split:
        heights = jnp.exp(jax.random.uniform(jax.random.fold_in(own, dim), (shards_of,), jnp.float32, low / len(split), high / len(split)))
        factor_of = factor_of * jnp.repeat(heights, shape[dim] // shards_of).reshape([-1 if axis == dim else 1 for axis in range(len(shape))])
    return factor_of


def bell_draw(key, shape, scale, limit, shards=(), kind=jnp.bfloat16):
    entries = jax.random.normal(key, shape, jnp.float32) * scale
    if len(shards) > 0:
        entries = block_scale(key, shape, shards, -0.22, 0.18) * entries
    return jnp.clip(entries, min=-limit, max=limit).astype(kind)


def setup_inputs(seed: int = 0, part: int = 0) -> dict:
    keys = jax.random.split(jax.random.key(seed), 8)
    own_keys = jax.random.split(jax.random.fold_in(keys[7], part), 8)
    features = bell_draw(own_keys[0], (F, H, W, C), 1.0, 6.0, ((0, 4), (1, 4)))
    space_kernel = bell_draw(keys[1], (3, 3, C, C), (9 * C) ** -0.5, 0.125)
    space_gain = jnp.clip(jnp.exp(jax.random.uniform(keys[2], (C,), jnp.float32, math.log(0.5), math.log(2.0))), 0.5, 2.0)
    space_bias = bell_draw(keys[3], (C,), 0.5, 3.0, (), jnp.float32)
    time_kernel = bell_draw(keys[4], (3, C, C), (3 * C) ** -0.5, 0.21875)
    time_gain = jnp.clip(jnp.exp(jax.random.uniform(keys[5], (C,), jnp.float32, math.log(0.5), math.log(2.0))), 0.5, 2.0)
    time_bias = bell_draw(keys[6], (C,), 0.5, 3.0, (), jnp.float32)
    return {"features": features, "space_kernel": space_kernel, "space_gain": space_gain, "space_bias": space_bias, "time_kernel": time_kernel, "time_gain": time_gain, "time_bias": time_bias}


def rms_silu(values, gain_vector):
    widened = values.astype(jnp.float32)
    scaled = widened * lax.rsqrt(lax.optimization_barrier(jnp.mean(widened * widened, axis=-1, keepdims=True)) + 1e-06) * gain_vector
    return jax.nn.silu(scaled).astype(jnp.bfloat16)

def spatial_frame(normed_frame, kernel):
    rows_count, cols_count, channels = normed_frame.shape
    padded = jnp.pad(normed_frame, ((1, 1), (1, 1), (0, 0)))
    summed = jnp.zeros((rows_count * cols_count, kernel.shape[3]), jnp.float32)
    for tap_row in range(3):
        for tap_col in range(3):
            window = padded[tap_row:tap_row + rows_count, tap_col:tap_col + cols_count].reshape(-1, channels)
            summed = summed + jnp.dot(window, kernel[tap_row, tap_col], preferred_element_type=jnp.float32)
    return summed.reshape(rows_count, cols_count, -1)

def reference(features, space_kernel, space_gain, space_bias, time_kernel, time_gain, time_bias):
    normed = rms_silu(features, space_gain)
    spatial = lax.map(lambda frame_data: spatial_frame(frame_data, space_kernel), normed)
    hidden = (features.astype(jnp.float32) + spatial + space_bias).astype(jnp.bfloat16)
    hidden = lax.optimization_barrier(hidden)
    normed_time = rms_silu(hidden, time_gain)
    frame_count = normed_time.shape[0]
    channels = normed_time.shape[-1]
    extended = jnp.pad(normed_time, ((2, 0), (0, 0), (0, 0), (0, 0)))
    summed = jnp.zeros((normed_time.size // channels, channels), jnp.float32)
    for time_lag in range(3):
        window = extended[2 - time_lag:2 - time_lag + frame_count].reshape(-1, channels)
        summed = summed + jnp.dot(window, time_kernel[time_lag], preferred_element_type=jnp.float32)
    temporal = summed.reshape(normed_time.shape).astype(jnp.bfloat16)
    temporal = lax.optimization_barrier(temporal)
    decoded = hidden.astype(jnp.float32) + temporal.astype(jnp.float32) + time_bias
    return decoded.astype(jnp.bfloat16)
```

```python
import functools

import jax
import jax.numpy as jnp
from jax import lax
from jax.experimental import pallas as pl
from jax.experimental.pallas import tpu as pltpu
from jax.sharding import PartitionSpec as P

LAGS = 2


def rms_silu(values, gain):
    mean = jnp.mean(values * values, axis=-1, keepdims=True)
    half = values * lax.rsqrt(mean + 1e-06) * (0.5 * gain)
    return half + half * jnp.tanh(half)


def dot(left, right):
    return jnp.dot(left, right, preferred_element_type=jnp.float32)


def group_starts(last):
    return sorted({min(max(1, start), last - 1) for start in (1, last - 5, last - 1)})


def kernel(
    features, space_kernel, space_gain, space_bias, time_kernel, time_gain, time_bias,
    out,
    feat, normed, hidden, ntime, earlier, partial, wspace, wtime, vectors,
    feat_sem, weight_sem, halo_send, halo_recv, time_send, time_recv,
):
    frames, rows, cols, channels = features.shape
    half = cols // 2
    last = rows - 1
    band, bands = lax.axis_index("band"), lax.axis_size("band")
    frame, frame_parts = lax.axis_index("frame"), lax.axis_size("frame")
    has_up, has_down = band > 0, band < bands - 1
    has_prev, has_next = frame > 0, frame < frame_parts - 1
    neighbours = (
        (has_up, {"band": band - 1}),
        (has_down, {"band": band + 1}),
        (has_prev, {"frame": frame - 1}),
        (has_next, {"frame": frame + 1}),
    )

    barrier = pltpu.get_barrier_semaphore()
    for present, device in neighbours:
        @pl.when(present)
        def _():
            pl.semaphore_signal(
                barrier, inc=1, device_id=device, device_id_type=pl.DeviceIdType.MESH
            )

    def row_copy(row, sem):
        return pltpu.make_async_copy(
            features.at[:, row], feat.at[row + 1], feat_sem.at[sem]
        )

    def rows_wait(start, count, sem):
        block = feat.at[pl.ds(start + 1, count)]
        pltpu.make_async_copy(block, block, feat_sem.at[sem]).wait()

    vector_copies = [
        pltpu.make_async_copy(vector, vectors.at[i], weight_sem.at[0])
        for i, vector in enumerate((space_gain, space_bias, time_gain, time_bias))
    ]
    vectors_copy = pltpu.make_async_copy(vectors, vectors, weight_sem.at[0])
    space_copy = pltpu.make_async_copy(space_kernel, wspace, weight_sem.at[1])
    lags_copy = pltpu.make_async_copy(time_kernel, wtime, weight_sem.at[2])
    for row in range(3):
        row_copy(row, 0).start()
    for copy in vector_copies:
        copy.start()
    space_copy.start()

    groups = group_starts(last)

    def time_copy(source, row, sem, left=0, width=cols):
        return pltpu.make_async_remote_copy(
            source.at[:, pl.ds(left, width)],
            earlier.at[row, :, pl.ds(left, width)],
            time_send.at[0],
            time_recv.at[sem],
            device_id={"frame": frame + 1},
            device_id_type=pl.DeviceIdType.MESH,
        )

    def row_send(row, sem, left=0, width=cols):
        source = ntime.at[row, pl.ds(frames - LAGS, LAGS)]
        pl.when(has_next)(time_copy(source, row, sem, left, width).start)

    def time_wait(block, sem):
        pl.when(has_prev)(
            pltpu.make_async_copy(block, block, time_recv.at[sem]).wait
        )

    def vector(i):
        return vectors[i].reshape(1, channels)

    def norm_part(slot, start=0, count=frames, left=0, width=cols):
        base = max(0, min(left - 16, cols - width - 16)) if width < cols else 0
        window = min(cols, width + 16)
        size = count * window
        values = feat[slot, start : start + count, base : base + window]
        result = rms_silu(values.reshape(size, channels).astype(jnp.float32), vector(0))
        column = base + lax.rem(
            lax.broadcasted_iota(jnp.int32, (size, channels), 0), window
        )
        before = jnp.where(column == 0, 0.0, pltpu.roll(result, 1, 0))
        after = jnp.where(column == cols - 1, 0.0, pltpu.roll(result, size - 1, 0))
        for i, piece in enumerate((before, result, after)):
            kept = piece.astype(jnp.bfloat16).reshape(count, window, channels)
            normed[
                slot, start : start + count, left : left + width,
                i * channels : (i + 1) * channels,
            ] = kept[:, left - base : left - base + width]

    def space_part(row, start=0, count=frames, left=0, width=cols):
        where = (slice(start, start + count), slice(left, left + width))
        size = count * width
        total = None
        for i in range(3):
            product = dot(
                normed[(row + i, *where)].reshape(size, 3 * channels),
                wspace[i].reshape(3 * channels, channels),
            )
            total = product if total is None else total + product
        centre = feat[(row + 1, *where)].reshape(size, channels).astype(jnp.float32)
        kept = (centre + total + vector(1)).astype(jnp.bfloat16)
        shape = (count, width, channels)
        hidden[(row, *where)] = kept.reshape(shape)
        ntime[(row, *where)] = (
            rms_silu(kept.astype(jnp.float32), vector(2)).astype(jnp.bfloat16).reshape(shape)
        )

    def own_totals(row):
        own = ntime[row]
        totals = [
            dot(own.reshape(-1, channels), wtime[0]).reshape(own.shape)[f]
            for f in range(frames)
        ]
        for lag in range(1, min(LAGS, frames - 1) + 1):
            term = dot(own[: frames - lag].reshape(-1, channels), wtime[lag])
            for f in range(lag, frames):
                totals[f] += term[(f - lag) * cols : (f - lag + 1) * cols]
        return totals

    def finish(row, f, total, left=0, width=cols):
        columns = slice(left, left + width)
        temporal = total.astype(jnp.bfloat16).astype(jnp.float32)
        kept = hidden[row, f, columns].astype(jnp.float32)
        out[f, row, columns] = (kept + temporal + vector(3)).astype(jnp.bfloat16)

    def time_part(row):
        totals = own_totals(row)
        for lag in range(1, LAGS + 1):
            past = earlier[row, LAGS - lag :]
            term = dot(past.reshape(-1, channels), wtime[lag])
            for f in range(lag):
                totals[f] += term[f * cols : (f + 1) * cols]
        for f in range(frames):
            finish(row, f, totals[f])

    def lag_sums(row):
        for f in range(LAGS):
            total = None
            for lag in range(f + 1, LAGS + 1):
                term = dot(ntime[row, frames - lag + f], wtime[lag])
                total = term if total is None else total + term
            partial[f] = total.astype(jnp.bfloat16)

    @pl.when(jnp.logical_not(has_prev))
    def _():
        earlier[...] = jnp.zeros_like(earlier)

    @pl.when(jnp.logical_not(has_up))
    def _():
        feat[0] = jnp.zeros(feat.shape[1:], feat.dtype)

    @pl.when(jnp.logical_not(has_down))
    def _():
        feat[rows + 1] = jnp.zeros(feat.shape[1:], feat.dtype)

    vectors_copy.wait()
    rows_wait(0, 3, 0)
    for slot in (1, 2, 3):
        norm_part(slot, 0, frames, 0, half)
    space_copy.wait()
    for row in range(3, rows):
        row_copy(row, 1 if row == 3 else 2).start()
    lags_copy.start()
    space_part(1, 0, frames, 0, half)

    peers = (
        (band + bands - 1) // bands
        + 1 - (band + 1) // bands
        + (frame + frame_parts - 1) // frame_parts
        + 1 - (frame + 1) // frame_parts
    )
    pl.semaphore_wait(barrier, peers)

    to_up = pltpu.make_async_remote_copy(
        features.at[:, 0], feat.at[rows + 1], halo_send.at[0], halo_recv.at[0],
        device_id={"band": band - 1}, device_id_type=pl.DeviceIdType.MESH,
    )
    to_down = pltpu.make_async_remote_copy(
        features.at[:, rows - 1], feat.at[0], halo_send.at[1], halo_recv.at[1],
        device_id={"band": band + 1}, device_id_type=pl.DeviceIdType.MESH,
    )
    pl.when(has_up)(to_up.start)
    pl.when(has_down)(to_down.start)

    row_send(1, 0, 0, half)
    for slot in (1, 2, 3):
        norm_part(slot, 0, frames, half, cols - half)
    space_part(1, 0, frames, half, cols - half)
    row_send(1, 0, half, cols - half)
    rows_wait(3, 1, 1)
    norm_part(4)
    space_part(2)
    row_send(2, 0)
    rows_wait(4, rows - 4, 2)

    @pl.loop(3, last)
    def _(row):
        norm_part(row + 2)
        space_part(row)
        row_send(row, sum((row >= g).astype(jnp.int32) for g in groups[1:]))

    pl.when(has_up)(to_down.wait_recv)
    pl.when(has_down)(to_up.wait_recv)
    norm_part(0)
    space_part(0)
    row_send(0, len(groups))
    norm_part(rows + 1)
    space_part(last)
    lags_copy.wait()

    @pl.when(has_next)
    def _():
        lag_sums(last)
        for side in range(2):
            time_copy(
                partial, last, len(groups) + 1 + side, side * half, half
            ).start()

    @pl.loop(1, last)
    def _(row):
        for i, start in enumerate(groups):
            end = groups[i + 1] if i + 1 < len(groups) else last

            @pl.when(row == start)
            def _():
                time_wait(earlier.at[pl.ds(start, end - start)], i)

        time_part(row)

    time_wait(earlier.at[0], len(groups))
    time_part(0)
    totals = own_totals(last)
    for side in range(2):
        columns = slice(side * half, (side + 1) * half)
        time_wait(earlier.at[last, :, pl.ds(side * half, half)], len(groups) + 1 + side)
        for f in range(frames):
            total = totals[f][columns]
            if f < LAGS:
                total += earlier[last, f, columns].astype(jnp.float32)
            finish(last, f, total, side * half, half)

    pl.when(has_up)(to_up.wait_send)
    pl.when(has_down)(to_down.wait_send)

    @pl.when(has_next)
    def _():
        pltpu.make_async_copy(earlier, earlier, time_send.at[0]).wait()


def body(features, *rest):
    frames, rows, cols, channels = features.shape
    bf16 = jnp.bfloat16
    return pl.pallas_call(
        kernel,
        out_shape=jax.ShapeDtypeStruct(features.shape, bf16),
        in_specs=[pl.BlockSpec(memory_space=pltpu.HBM)] * 7,
        out_specs=pl.BlockSpec(memory_space=pltpu.VMEM),
        scratch_shapes=[
            pltpu.VMEM((rows + 2, frames, cols, channels), bf16),
            pltpu.VMEM((rows + 2, frames, cols, 3 * channels), bf16),
            pltpu.VMEM((rows, frames, cols, channels), bf16),
            pltpu.VMEM((rows, frames, cols, channels), bf16),
            pltpu.VMEM((rows, LAGS, cols, channels), bf16),
            pltpu.VMEM((LAGS, cols, channels), bf16),
            pltpu.VMEM(rest[0].shape, bf16),
            pltpu.VMEM(rest[3].shape, bf16),
            pltpu.VMEM((4, channels), jnp.float32),
            pltpu.SemaphoreType.DMA((3,)),
            pltpu.SemaphoreType.DMA((3,)),
            pltpu.SemaphoreType.DMA((2,)),
            pltpu.SemaphoreType.DMA((2,)),
            pltpu.SemaphoreType.DMA((1,)),
            pltpu.SemaphoreType.DMA((len(group_starts(rows - 1)) + 3,)),
        ],
        compiler_params=pltpu.CompilerParams(
            collective_id=0, has_side_effects=True, vmem_limit_bytes=36 * 1024 * 1024
        ),
    )(*[pltpu.with_memory_space_constraint(x, pltpu.HBM) for x in (features, *rest)])


def solution(mesh):
    return jax.shard_map(
        body,
        mesh=mesh,
        in_specs=(P(("grp", "frame"), "band", None, None), P(), P(), P(), P(), P(), P()),
        out_specs=P(("grp", "frame"), "band", None, None),
        check_vma=False,
    )
```

```python
import functools

import jax
import jax.numpy as jnp
from jax import lax
from jax.experimental import pallas as pl
from jax.experimental.pallas import tpu as pltpu
from jax.sharding import PartitionSpec as P

LAGS = 2


def rms_silu(values, gain):
    mean = jnp.mean(values * values, axis=-1, keepdims=True)
    half = values * lax.rsqrt(mean + 1e-06) * (0.5 * gain)
    return half + half * jnp.tanh(half)


def dot(left, right):
    return jnp.dot(left, right, preferred_element_type=jnp.float32)


def group_starts(last):
    return sorted({min(max(1, start), last - 1) for start in (1, last - 5, last - 1)})


def kernel(
    features, space_kernel, space_gain, space_bias, time_kernel, time_gain, time_bias,
    out,
    feat, normed, hidden, ntime, earlier, partial, wspace, wtime, vectors,
    feat_sem, weight_sem, halo_send, halo_recv, time_send, time_recv,
):
    frames, rows, cols, channels = features.shape
    half = cols // 2
    split = frames - LAGS + 1
    last = rows - 1
    band, bands = lax.axis_index("band"), lax.axis_size("band")
    frame, frame_parts = lax.axis_index("frame"), lax.axis_size("frame")
    has_up, has_down = band > 0, band < bands - 1
    has_prev, has_next = frame > 0, frame < frame_parts - 1
    neighbours = (
        (has_up, {"band": band - 1}),
        (has_down, {"band": band + 1}),
        (has_prev, {"frame": frame - 1}),
        (has_next, {"frame": frame + 1}),
    )

    barrier = pltpu.get_barrier_semaphore()

    def greet(present, device):
        @pl.when(present)
        def _():
            pl.semaphore_signal(
                barrier, inc=1, device_id=device, device_id_type=pl.DeviceIdType.MESH
            )

    def rows_start(first, count, sem, start=0, size=frames, step=None):
        step = step or count
        for f in range(start, start + size):
            for row in range(first, first + count, step):
                pltpu.make_async_copy(
                    features.at[f, pl.ds(row, step)],
                    feat.at[pl.ds(row + 1, step), f],
                    feat_sem.at[sem],
                ).start()

    def rows_wait(first, count, sem, start=0, size=frames):
        block = feat.at[pl.ds(first + 1, count), pl.ds(start, size)]
        pltpu.make_async_copy(block, block, feat_sem.at[sem]).wait()

    vector_copies = [
        pltpu.make_async_copy(vector, vectors.at[i], weight_sem.at[0])
        for i, vector in enumerate((space_gain, space_bias, time_gain, time_bias))
    ]
    vectors_copy = pltpu.make_async_copy(vectors, vectors, weight_sem.at[0])
    space_copies = [
        pltpu.make_async_copy(space_kernel.at[i], wspace.at[i], weight_sem.at[1 + i])
        for i in range(3)
    ]
    lags_copy = pltpu.make_async_copy(time_kernel, wtime, weight_sem.at[4])
    rows_start(0, 3, 0, 0, split, 1)
    for copy in vector_copies:
        copy.start()
    greet(*neighbours[2])
    for copy in space_copies:
        copy.start()
    for i in (0, 1, 3):
        greet(*neighbours[i])
    rows_start(0, 4, 1, split, frames - split)
    rows_start(3, 1, 2, 0, split)

    groups = group_starts(last)

    def time_copy(source, target, sem):
        return pltpu.make_async_remote_copy(
            source,
            target,
            time_send.at[0],
            time_recv.at[sem],
            device_id={"frame": frame + 1},
            device_id_type=pl.DeviceIdType.MESH,
        )

    def row_send(row, sem, start=0, count=LAGS):
        source = ntime.at[row, pl.ds(frames - LAGS + start, count)]
        target = earlier.at[row, pl.ds(start, count)]
        pl.when(has_next)(time_copy(source, target, sem).start)

    def time_wait(block, sem):
        pl.when(has_prev)(
            pltpu.make_async_copy(block, block, time_recv.at[sem]).wait
        )

    def vector(i):
        return vectors[i].reshape(1, channels)

    def norm_part(slot, start=0, count=frames):
        size = count * cols
        values = feat[slot, start : start + count]
        result = rms_silu(values.reshape(size, channels).astype(jnp.float32), vector(0))
        column = lax.rem(lax.broadcasted_iota(jnp.int32, (size, channels), 0), cols)
        before = jnp.where(column == 0, 0.0, pltpu.roll(result, 1, 0))
        after = jnp.where(column == cols - 1, 0.0, pltpu.roll(result, size - 1, 0))
        for i, piece in enumerate((before, result, after)):
            normed[
                slot, start : start + count, :, i * channels : (i + 1) * channels
            ] = piece.astype(jnp.bfloat16).reshape(count, cols, channels)

    def taps(block, chosen, start, count):
        total = None
        for i, low, high in chosen:
            columns = slice(low * channels, high * channels)
            parts = [
                normed[row + i, start : start + count, :, columns]
                for row in block
            ]
            parts = [part.reshape(-1, (high - low) * channels) for part in parts]
            left = parts[0] if len(parts) == 1 else jnp.concatenate(parts, 0)
            term = dot(left, wspace[i, low:high].reshape(-1, channels))
            total = term if total is None else total + term
        return total

    def space_store(block, total, start, count):
        size = count * cols
        shape = (count, cols, channels)
        where = slice(start, start + count)
        for i, row in enumerate(block):
            centre = feat[row + 1, where].reshape(size, channels).astype(jnp.float32)
            summed = centre + total[i * size : (i + 1) * size] + vector(1)
            kept = summed.astype(jnp.bfloat16)
            hidden[row, where] = kept.reshape(shape)
            after = rms_silu(kept.astype(jnp.float32), vector(2))
            ntime[row, where] = after.astype(jnp.bfloat16).reshape(shape)

    def space_part(block, start=0, count=frames):
        total = taps(block, ((0, 0, 3), (1, 0, 3), (2, 0, 3)), start, count)
        space_store(block, total, start, count)

    def once(step):
        pl.loop(0, 1 + band // bands)(lambda _: step())

    def own_totals(row):
        own = ntime[row]
        totals = [
            dot(own.reshape(-1, channels), wtime[0]).reshape(own.shape)[f]
            for f in range(frames)
        ]
        for lag in range(1, min(LAGS, frames - 1) + 1):
            term = dot(own[: frames - lag].reshape(-1, channels), wtime[lag])
            for f in range(lag, frames):
                totals[f] += term[(f - lag) * cols : (f - lag + 1) * cols]
        return totals

    def finish(row, f, total, left=0, width=cols):
        columns = slice(left, left + width)
        temporal = total.astype(jnp.bfloat16).astype(jnp.float32)
        kept = hidden[row, f, columns].astype(jnp.float32)
        out[f, row, columns] = (kept + temporal + vector(3)).astype(jnp.bfloat16)

    def time_part(row):
        totals = own_totals(row)
        for lag in range(1, LAGS + 1):
            past = earlier[row, LAGS - lag :]
            term = dot(past.reshape(-1, channels), wtime[lag])
            for f in range(lag):
                totals[f] += term[f * cols : (f + 1) * cols]
        for f in range(frames):
            finish(row, f, totals[f])

    def lag_sums(row):
        for f in range(LAGS):
            total = None
            for lag in range(f + 1, LAGS + 1):
                term = dot(ntime[row, frames - lag + f], wtime[lag])
                total = term if total is None else total + term
            partial[f] = total.astype(jnp.bfloat16)

    @pl.when(jnp.logical_not(has_prev))
    def _():
        earlier[...] = jnp.zeros_like(earlier)

    @pl.when(jnp.logical_not(has_up))
    def _():
        feat[0] = jnp.zeros(feat.shape[1:], feat.dtype)

    @pl.when(jnp.logical_not(has_down))
    def _():
        feat[rows + 1] = jnp.zeros(feat.shape[1:], feat.dtype)

    vectors_copy.wait()
    rows_wait(0, 3, 0, 0, split)
    for slot in (1, 2, 3):
        norm_part(slot, 0, split)
    space_copies[0].wait()

    @once
    def _():
        total = taps((1,), ((0, 0, 3),), 0, split)
        space_copies[1].wait()
        total += taps((1,), ((1, 0, 3),), 0, split)
        space_copies[2].wait()
        space_store((1,), total + taps((1,), ((2, 0, 3),), 0, split), 0, split)

    peers = (
        (band + bands - 1) // bands
        + 1 - (band + 1) // bands
        + (frame + frame_parts - 1) // frame_parts
        + 1 - (frame + 1) // frame_parts
    )
    pl.semaphore_wait(barrier, peers)

    to_up = pltpu.make_async_remote_copy(
        features.at[:, 0], feat.at[rows + 1], halo_send.at[0], halo_recv.at[0],
        device_id={"band": band - 1}, device_id_type=pl.DeviceIdType.MESH,
    )
    to_down = pltpu.make_async_remote_copy(
        features.at[:, rows - 1], feat.at[0], halo_send.at[1], halo_recv.at[1],
        device_id={"band": band + 1}, device_id_type=pl.DeviceIdType.MESH,
    )
    pl.when(has_up)(to_up.start)
    pl.when(has_down)(to_down.start)

    row_send(1, 0, 0, 1)
    rows_start(4, rows - 4, 3)
    lags_copy.start()
    rows_wait(0, 4, 1, split, frames - split)
    rows_wait(3, 1, 2, 0, split)

    @once
    def _():
        for slot in (1, 2, 3, 4):
            norm_part(slot, split, frames - split)
        space_part((1, 2), split, frames - split)

    for row in (1, 2):
        row_send(row, 0, 1, LAGS - 1)

    @once
    def _():
        norm_part(4, 0, split)
        space_part((2,), 0, split)

    row_send(2, 0, 0, 1)
    rows_wait(4, rows - 4, 3)

    @pl.loop(3, last)
    def _(row):
        norm_part(row + 2)
        space_part((row,))
        row_send(row, sum((row >= g).astype(jnp.int32) for g in groups[1:]))

    pl.when(has_up)(to_down.wait_recv)
    pl.when(has_down)(to_up.wait_recv)

    @once
    def _():
        norm_part(0)
        space_part((0,))

    row_send(0, len(groups))

    @once
    def _():
        norm_part(rows + 1)
        space_part((last,))

    lags_copy.wait()

    @pl.when(has_next)
    def _():
        lag_sums(last)
        for side in range(2):
            columns = pl.ds(side * half, half)
            time_copy(
                partial.at[:, columns],
                earlier.at[last, :, columns],
                len(groups) + 1 + side,
            ).start()

    @pl.loop(1, last)
    def _(row):
        for i, start in enumerate(groups):
            end = groups[i + 1] if i + 1 < len(groups) else last

            @pl.when(row == start)
            def _():
                time_wait(earlier.at[pl.ds(start, end - start)], i)

        time_part(row)

    time_wait(earlier.at[0], len(groups))
    time_part(0)
    totals = own_totals(last)
    for side in range(2):
        columns = slice(side * half, (side + 1) * half)
        time_wait(earlier.at[last, :, pl.ds(side * half, half)], len(groups) + 1 + side)
        for f in range(frames):
            total = totals[f][columns]
            if f < LAGS:
                total += earlier[last, f, columns].astype(jnp.float32)
            finish(last, f, total, side * half, half)

    pl.when(has_up)(to_up.wait_send)
    pl.when(has_down)(to_down.wait_send)

    @pl.when(has_next)
    def _():
        pltpu.make_async_copy(earlier, earlier, time_send.at[0]).wait()


def body(features, *rest):
    frames, rows, cols, channels = features.shape
    bf16 = jnp.bfloat16
    return pl.pallas_call(
        kernel,
        out_shape=jax.ShapeDtypeStruct(features.shape, bf16),
        in_specs=[pl.BlockSpec(memory_space=pltpu.HBM)] * 7,
        out_specs=pl.BlockSpec(memory_space=pltpu.VMEM),
        scratch_shapes=[
            pltpu.VMEM((rows + 2, frames, cols, channels), bf16),
            pltpu.VMEM((rows + 2, frames, cols, 3 * channels), bf16),
            pltpu.VMEM((rows, frames, cols, channels), bf16),
            pltpu.VMEM((rows, frames, cols, channels), bf16),
            pltpu.VMEM((rows, LAGS, cols, channels), bf16),
            pltpu.VMEM((LAGS, cols, channels), bf16),
            pltpu.VMEM(rest[0].shape, bf16),
            pltpu.VMEM(rest[3].shape, bf16),
            pltpu.VMEM((4, channels), jnp.float32),
            pltpu.SemaphoreType.DMA((4,)),
            pltpu.SemaphoreType.DMA((5,)),
            pltpu.SemaphoreType.DMA((2,)),
            pltpu.SemaphoreType.DMA((2,)),
            pltpu.SemaphoreType.DMA((1,)),
            pltpu.SemaphoreType.DMA((len(group_starts(rows - 1)) + 3,)),
        ],
        compiler_params=pltpu.CompilerParams(
            collective_id=0, has_side_effects=True, vmem_limit_bytes=36 * 1024 * 1024
        ),
    )(*[pltpu.with_memory_space_constraint(x, pltpu.HBM) for x in (features, *rest)])


def solution(mesh):
    return jax.shard_map(
        body,
        mesh=mesh,
        in_specs=(P(("grp", "frame"), "band", None, None), P(), P(), P(), P(), P(), P()),
        out_specs=P(("grp", "frame"), "band", None, None),
        check_vma=False,
    )
```

```python
import functools

import jax
import jax.numpy as jnp
from jax import lax
from jax.experimental import pallas as pl
from jax.experimental.pallas import tpu as pltpu
from jax.sharding import PartitionSpec as P

LAGS = 2


def rms_silu(values, gain):
    mean = jnp.mean(values * values, axis=-1, keepdims=True)
    half = values * lax.rsqrt(mean + 1e-06) * (0.5 * gain)
    return half + half * jnp.tanh(half)


def dot(left, right):
    return jnp.dot(left, right, preferred_element_type=jnp.float32)


def group_starts(last):
    return sorted({min(max(1, start), last - 1) for start in (1, last - 5, last - 1)})


def kernel(
    features, space_kernel, space_gain, space_bias, time_kernel, time_gain, time_bias,
    out,
    feat, normed, hidden, ntime, earlier, partial, wspace, wtime, vectors,
    feat_sem, weight_sem, halo_send, halo_recv, time_send, time_recv,
):
    frames, rows, cols, channels = features.shape
    half = cols // 2
    split = frames - LAGS + 1
    last = rows - 1
    band, bands = lax.axis_index("band"), lax.axis_size("band")
    frame, frame_parts = lax.axis_index("frame"), lax.axis_size("frame")
    has_up, has_down = band > 0, band < bands - 1
    has_prev, has_next = frame > 0, frame < frame_parts - 1
    neighbours = (
        (has_up, {"band": band - 1}),
        (has_down, {"band": band + 1}),
        (has_prev, {"frame": frame - 1}),
        (has_next, {"frame": frame + 1}),
    )

    barrier = pltpu.get_barrier_semaphore()

    def greet(present, device):
        @pl.when(present)
        def _():
            pl.semaphore_signal(
                barrier, inc=1, device_id=device, device_id_type=pl.DeviceIdType.MESH
            )

    def rows_start(first, count, sem, start=0, size=frames, step=None):
        step = step or count
        for f in range(start, start + size):
            for row in range(first, first + count, step):
                pltpu.make_async_copy(
                    features.at[f, pl.ds(row, step)],
                    feat.at[pl.ds(row + 1, step), f],
                    feat_sem.at[sem],
                ).start()

    def rows_wait(first, count, sem, start=0, size=frames):
        block = feat.at[pl.ds(first + 1, count), pl.ds(start, size)]
        pltpu.make_async_copy(block, block, feat_sem.at[sem]).wait()

    vector_copies = [
        pltpu.make_async_copy(vector, vectors.at[i], weight_sem.at[0])
        for i, vector in enumerate((space_gain, space_bias, time_gain, time_bias))
    ]
    vectors_copy = pltpu.make_async_copy(vectors, vectors, weight_sem.at[0])
    space_copies = [
        pltpu.make_async_copy(
            space_kernel.at[pl.ds(start, count)],
            wspace.at[pl.ds(start, count)],
            weight_sem.at[sem],
        )
        for start, count, sem in ((0, 2, 1), (2, 1, 2))
    ]
    lags_copy = pltpu.make_async_copy(time_kernel, wtime, weight_sem.at[3])
    rows_start(0, 3, 0, 0, split, 1)
    for copy in vector_copies:
        copy.start()
    greet(*neighbours[2])
    for copy in space_copies:
        copy.start()
    for i in (0, 1, 3):
        greet(*neighbours[i])
    rows_start(0, 4, 1, split, frames - split)
    rows_start(3, 1, 2, 0, split)

    groups = group_starts(last)

    def time_copy(source, target, sem):
        return pltpu.make_async_remote_copy(
            source,
            target,
            time_send.at[0],
            time_recv.at[sem],
            device_id={"frame": frame + 1},
            device_id_type=pl.DeviceIdType.MESH,
        )

    def row_send(row, sem, start=0, count=LAGS):
        source = ntime.at[row, pl.ds(frames - LAGS + start, count)]
        target = earlier.at[row, pl.ds(start, count)]
        pl.when(has_next)(time_copy(source, target, sem).start)

    def time_wait(block, sem):
        pl.when(has_prev)(
            pltpu.make_async_copy(block, block, time_recv.at[sem]).wait
        )

    def vector(i):
        return vectors[i].reshape(1, channels)

    def norm_part(slot, start=0, count=frames):
        size = count * cols
        values = feat[slot, start : start + count]
        result = rms_silu(values.reshape(size, channels).astype(jnp.float32), vector(0))
        column = lax.rem(lax.broadcasted_iota(jnp.int32, (size, channels), 0), cols)
        before = jnp.where(column == 0, 0.0, pltpu.roll(result, 1, 0))
        after = jnp.where(column == cols - 1, 0.0, pltpu.roll(result, size - 1, 0))
        for i, piece in enumerate((before, result, after)):
            normed[
                slot, start : start + count, :, i * channels : (i + 1) * channels
            ] = piece.astype(jnp.bfloat16).reshape(count, cols, channels)

    def taps(block, chosen, start, count):
        total = None
        for i, low, high in chosen:
            columns = slice(low * channels, high * channels)
            parts = [
                normed[row + i, start : start + count, :, columns]
                for row in block
            ]
            parts = [part.reshape(-1, (high - low) * channels) for part in parts]
            left = parts[0] if len(parts) == 1 else jnp.concatenate(parts, 0)
            term = dot(left, wspace[i, low:high].reshape(-1, channels))
            total = term if total is None else total + term
        return total

    def space_store(row, total, start, count):
        shape = (count, cols, channels)
        where = slice(start, start + count)
        centre = feat[row + 1, where].reshape(-1, channels).astype(jnp.float32)
        kept = (centre + total + vector(1)).astype(jnp.bfloat16)
        hidden[row, where] = kept.reshape(shape)
        after = rms_silu(kept.astype(jnp.float32), vector(2))
        ntime[row, where] = after.astype(jnp.bfloat16).reshape(shape)

    def space_part(block, start=0, count=frames, stored=lambda row: None):
        total = taps(block, ((0, 0, 3), (1, 0, 3), (2, 0, 3)), start, count)
        size = count * cols
        for i, row in enumerate(block):
            space_store(row, total[i * size : (i + 1) * size], start, count)
            stored(row)

    def once(step):
        pl.loop(0, 1 + band // bands)(lambda _: step())

    def own_totals(row):
        own = ntime[row]
        totals = [
            dot(own.reshape(-1, channels), wtime[0]).reshape(own.shape)[f]
            for f in range(frames)
        ]
        for lag in range(1, min(LAGS, frames - 1) + 1):
            term = dot(own[: frames - lag].reshape(-1, channels), wtime[lag])
            for f in range(lag, frames):
                totals[f] += term[(f - lag) * cols : (f - lag + 1) * cols]
        return totals

    def finish(row, f, total, left=0, width=cols):
        columns = slice(left, left + width)
        temporal = total.astype(jnp.bfloat16).astype(jnp.float32)
        kept = hidden[row, f, columns].astype(jnp.float32)
        out[f, row, columns] = (kept + temporal + vector(3)).astype(jnp.bfloat16)

    def time_part(row):
        totals = own_totals(row)
        for lag in range(1, LAGS + 1):
            past = earlier[row, LAGS - lag :]
            term = dot(past.reshape(-1, channels), wtime[lag])
            for f in range(lag):
                totals[f] += term[f * cols : (f + 1) * cols]
        for f in range(frames):
            finish(row, f, totals[f])

    def lag_sums(row):
        for f in range(LAGS):
            total = None
            for lag in range(f + 1, LAGS + 1):
                term = dot(ntime[row, frames - lag + f], wtime[lag])
                total = term if total is None else total + term
            partial[f] = total.astype(jnp.bfloat16)

    @pl.when(jnp.logical_not(has_prev))
    def _():
        earlier[...] = jnp.zeros_like(earlier)

    @pl.when(jnp.logical_not(has_up))
    def _():
        feat[0] = jnp.zeros(feat.shape[1:], feat.dtype)

    @pl.when(jnp.logical_not(has_down))
    def _():
        feat[rows + 1] = jnp.zeros(feat.shape[1:], feat.dtype)

    vectors_copy.wait()
    rows_wait(0, 3, 0, 0, split)
    for slot in (1, 2, 3):
        norm_part(slot, 0, split)
    space_copies[0].wait()

    @once
    def _():
        total = taps((1,), ((0, 0, 3), (1, 0, 3)), 0, split)
        space_copies[1].wait()
        space_store(1, total + taps((1,), ((2, 0, 3),), 0, split), 0, split)

    peers = (
        (band + bands - 1) // bands
        + 1 - (band + 1) // bands
        + (frame + frame_parts - 1) // frame_parts
        + 1 - (frame + 1) // frame_parts
    )
    pl.semaphore_wait(barrier, peers)

    row_send(1, 0, 0, 1)
    to_up = pltpu.make_async_remote_copy(
        features.at[:, 0], feat.at[rows + 1], halo_send.at[0], halo_recv.at[0],
        device_id={"band": band - 1}, device_id_type=pl.DeviceIdType.MESH,
    )
    to_down = pltpu.make_async_remote_copy(
        features.at[:, rows - 1], feat.at[0], halo_send.at[1], halo_recv.at[1],
        device_id={"band": band + 1}, device_id_type=pl.DeviceIdType.MESH,
    )
    pl.when(has_up)(to_up.start)
    pl.when(has_down)(to_down.start)

    rows_start(4, rows - 4, 3)
    lags_copy.start()
    rows_wait(0, 4, 1, split, frames - split)
    rows_wait(3, 1, 2, 0, split)

    @once
    def _():
        for slot in (1, 2, 3, 4):
            norm_part(slot, split, frames - split)
        space_part(
            (1, 2), split, frames - split, lambda row: row_send(row, 0, 1, LAGS - 1)
        )

    @once
    def _():
        norm_part(4, 0, split)
        space_part((2,), 0, split)

    row_send(2, 0, 0, 1)
    rows_wait(4, rows - 4, 3)

    @pl.loop(3, last)
    def _(row):
        norm_part(row + 2)
        space_part((row,))
        row_send(row, sum((row >= g).astype(jnp.int32) for g in groups[1:]))

    pl.when(has_up)(to_down.wait_recv)
    pl.when(has_down)(to_up.wait_recv)

    @once
    def _():
        norm_part(0)
        space_part((0,))

    row_send(0, len(groups))

    @once
    def _():
        norm_part(rows + 1)
        space_part((last,))

    lags_copy.wait()

    @pl.when(has_next)
    def _():
        lag_sums(last)
        for side in range(2):
            columns = pl.ds(side * half, half)
            time_copy(
                partial.at[:, columns],
                earlier.at[last, :, columns],
                len(groups) + 1 + side,
            ).start()

    @pl.loop(1, last)
    def _(row):
        for i, start in enumerate(groups):
            end = groups[i + 1] if i + 1 < len(groups) else last

            @pl.when(row == start)
            def _():
                time_wait(earlier.at[pl.ds(start, end - start)], i)

        time_part(row)

    time_wait(earlier.at[0], len(groups))
    time_part(0)
    totals = own_totals(last)
    for side in range(2):
        columns = slice(side * half, (side + 1) * half)
        time_wait(earlier.at[last, :, pl.ds(side * half, half)], len(groups) + 1 + side)
        for f in range(frames):
            total = totals[f][columns]
            if f < LAGS:
                total += earlier[last, f, columns].astype(jnp.float32)
            finish(last, f, total, side * half, half)

    pl.when(has_up)(to_up.wait_send)
    pl.when(has_down)(to_down.wait_send)

    @pl.when(has_next)
    def _():
        pltpu.make_async_copy(earlier, earlier, time_send.at[0]).wait()


def body(features, *rest):
    frames, rows, cols, channels = features.shape
    bf16 = jnp.bfloat16
    return pl.pallas_call(
        kernel,
        out_shape=jax.ShapeDtypeStruct(features.shape, bf16),
        in_specs=[pl.BlockSpec(memory_space=pltpu.HBM)] * 7,
        out_specs=pl.BlockSpec(memory_space=pltpu.VMEM),
        scratch_shapes=[
            pltpu.VMEM((rows + 2, frames, cols, channels), bf16),
            pltpu.VMEM((rows + 2, frames, cols, 3 * channels), bf16),
            pltpu.VMEM((rows, frames, cols, channels), bf16),
            pltpu.VMEM((rows, frames, cols, channels), bf16),
            pltpu.VMEM((rows, LAGS, cols, channels), bf16),
            pltpu.VMEM((LAGS, cols, channels), bf16),
            pltpu.VMEM(rest[0].shape, bf16),
            pltpu.VMEM(rest[3].shape, bf16),
            pltpu.VMEM((4, channels), jnp.float32),
            pltpu.SemaphoreType.DMA((4,)),
            pltpu.SemaphoreType.DMA((4,)),
            pltpu.SemaphoreType.DMA((2,)),
            pltpu.SemaphoreType.DMA((2,)),
            pltpu.SemaphoreType.DMA((1,)),
            pltpu.SemaphoreType.DMA((len(group_starts(rows - 1)) + 3,)),
        ],
        compiler_params=pltpu.CompilerParams(
            collective_id=0, has_side_effects=True, vmem_limit_bytes=36 * 1024 * 1024
        ),
    )(*[pltpu.with_memory_space_constraint(x, pltpu.HBM) for x in (features, *rest)])


def solution(mesh):
    return jax.shard_map(
        body,
        mesh=mesh,
        in_specs=(P(("grp", "frame"), "band", None, None), P(), P(), P(), P(), P(), P()),
        out_specs=P(("grp", "frame"), "band", None, None),
        check_vma=False,
    )
```

```python
import functools

import jax
import jax.numpy as jnp
from jax import lax
from jax.experimental import pallas as pl
from jax.experimental.pallas import tpu as pltpu
from jax.sharding import PartitionSpec as P

LAGS = 2


def rms_silu(values, gain):
    mean = jnp.mean(values * values, axis=-1, keepdims=True)
    half = values * lax.rsqrt(mean + 1e-06) * (0.5 * gain)
    return half + half * jnp.tanh(half)


def dot(left, right):
    return jnp.dot(left, right, preferred_element_type=jnp.float32)


def group_starts(last):
    return sorted({min(max(1, start), last - 1) for start in (1, last - 5, last - 1)})


def kernel(
    features, space_kernel, space_gain, space_bias, time_kernel, time_gain, time_bias,
    out,
    feat, normed, begun, hidden, ntime, earlier, partial, wspace, wtime, vectors,
    feat_sem, weight_sem, halo_recv, time_recv,
):
    frames, rows, cols, channels = features.shape
    half = cols // 2
    split = frames - LAGS + 1
    last = rows - 1
    band, bands = lax.axis_index("band"), lax.axis_size("band")
    frame, frame_parts = lax.axis_index("frame"), lax.axis_size("frame")
    has_up, has_down = band > 0, band < bands - 1
    has_prev, has_next = frame > 0, frame < frame_parts - 1
    neighbours = (
        (has_up, {"band": band - 1}),
        (has_down, {"band": band + 1}),
        (has_prev, {"frame": frame - 1}),
        (has_next, {"frame": frame + 1}),
    )

    barrier = pltpu.get_barrier_semaphore()

    def greet(present, device):
        @pl.when(present)
        def _():
            pl.semaphore_signal(
                barrier, inc=1, device_id=device, device_id_type=pl.DeviceIdType.MESH
            )

    def rows_start(first, count, sem, start=0, size=frames, step=None):
        step = step or count
        for f in range(start, start + size):
            for row in range(first, first + count, step):
                pltpu.make_async_copy(
                    features.at[f, pl.ds(row, step)],
                    feat.at[pl.ds(row + 1, step), f],
                    feat_sem.at[sem],
                ).start()

    def rows_wait(first, count, sem, start=0, size=frames):
        block = feat.at[pl.ds(first + 1, count), pl.ds(start, size)]
        pltpu.make_async_copy(block, block, feat_sem.at[sem]).wait()

    vector_copies = [
        pltpu.make_async_copy(vector, vectors.at[i], weight_sem.at[0])
        for i, vector in enumerate((space_gain, space_bias, time_gain, time_bias))
    ]
    vectors_copy = pltpu.make_async_copy(vectors, vectors, weight_sem.at[0])
    space_copies = [
        pltpu.make_async_copy(
            space_kernel.at[pl.ds(start, count)],
            wspace.at[pl.ds(start, count)],
            weight_sem.at[sem],
        )
        for start, count, sem in ((0, 2, 1), (2, 1, 2))
    ]
    lags_copy = pltpu.make_async_copy(time_kernel, wtime, feat_sem.at[2])
    rows_start(0, 3, 0, 0, split, 1)
    for copy in vector_copies:
        copy.start()
    greet(*neighbours[2])
    for copy in space_copies:
        copy.start()
    for i in (0, 1, 3):
        greet(*neighbours[i])
    rows_start(0, 4, 1, split, frames - split)
    rows_start(3, 1, 2, 0, split)

    time_send, up_send, down_send = (weight_sem.at[i] for i in range(3))
    groups = group_starts(last)

    def time_copy(source, target, sem):
        return pltpu.make_async_remote_copy(
            source,
            target,
            time_send,
            time_recv.at[sem],
            device_id={"frame": frame + 1},
            device_id_type=pl.DeviceIdType.MESH,
        )

    def row_send(row, sem, start=0, count=LAGS):
        source = ntime.at[row, pl.ds(frames - LAGS + start, count)]
        target = earlier.at[row, pl.ds(start, count)]
        pl.when(has_next)(time_copy(source, target, sem).start)

    def time_wait(block, sem):
        pl.when(has_prev)(
            pltpu.make_async_copy(block, block, time_recv.at[sem]).wait
        )

    def vector(i):
        return vectors[i].reshape(1, channels)

    def norm_part(slot, start=0, count=frames):
        size = count * cols
        values = feat[slot, start : start + count]
        result = rms_silu(values.reshape(size, channels).astype(jnp.float32), vector(0))
        column = lax.rem(lax.broadcasted_iota(jnp.int32, (size, channels), 0), cols)
        before = jnp.where(column == 0, 0.0, pltpu.roll(result, 1, 0))
        after = jnp.where(column == cols - 1, 0.0, pltpu.roll(result, size - 1, 0))
        for i, piece in enumerate((before, result, after)):
            normed[
                slot, start : start + count, :, i * channels : (i + 1) * channels
            ] = piece.astype(jnp.bfloat16).reshape(count, cols, channels)

    def taps(block, chosen, start, count):
        total = None
        for i, low, high in chosen:
            columns = slice(low * channels, high * channels)
            parts = [
                normed[row + i, start : start + count, :, columns]
                for row in block
            ]
            parts = [part.reshape(-1, (high - low) * channels) for part in parts]
            left = parts[0] if len(parts) == 1 else jnp.concatenate(parts, 0)
            term = dot(left, wspace[i, low:high].reshape(-1, channels))
            total = term if total is None else total + term
        return total

    def space_store(row, total, start, count):
        shape = (count, cols, channels)
        where = slice(start, start + count)
        centre = feat[row + 1, where].reshape(-1, channels).astype(jnp.float32)
        kept = (centre + total + vector(1)).astype(jnp.bfloat16)
        hidden[row, where] = kept.reshape(shape)
        after = rms_silu(kept.astype(jnp.float32), vector(2))
        ntime[row, where] = after.astype(jnp.bfloat16).reshape(shape)

    def space_part(block, start=0, count=frames, stored=lambda row: None):
        total = taps(block, ((0, 0, 3), (1, 0, 3), (2, 0, 3)), start, count)
        size = count * cols
        for i, row in enumerate(block):
            space_store(row, total[i * size : (i + 1) * size], start, count)
            stored(row)

    def once(step):
        pl.loop(0, 1 + band // bands)(lambda _: step())

    def own_totals(row):
        own = ntime[row]
        totals = [
            dot(own.reshape(-1, channels), wtime[0]).reshape(own.shape)[f]
            for f in range(frames)
        ]
        for lag in range(1, min(LAGS, frames - 1) + 1):
            term = dot(own[: frames - lag].reshape(-1, channels), wtime[lag])
            for f in range(lag, frames):
                totals[f] += term[(f - lag) * cols : (f - lag + 1) * cols]
        return totals

    def finish(row, f, total, left=0, width=cols):
        columns = slice(left, left + width)
        temporal = total.astype(jnp.bfloat16).astype(jnp.float32)
        kept = hidden[row, f, columns].astype(jnp.float32)
        out[f, row, columns] = (kept + temporal + vector(3)).astype(jnp.bfloat16)

    def time_part(row):
        totals = own_totals(row)
        for lag in range(1, LAGS + 1):
            past = earlier[row, LAGS - lag :]
            term = dot(past.reshape(-1, channels), wtime[lag])
            for f in range(lag):
                totals[f] += term[f * cols : (f + 1) * cols]
        for f in range(frames):
            finish(row, f, totals[f])

    def lag_sums(row):
        for f in range(LAGS):
            total = None
            for lag in range(f + 1, LAGS + 1):
                term = dot(ntime[row, frames - lag + f], wtime[lag])
                total = term if total is None else total + term
            partial[f] = total.astype(jnp.bfloat16)

    @pl.when(jnp.logical_not(has_prev))
    def _():
        earlier[...] = jnp.zeros_like(earlier)

    @pl.when(jnp.logical_not(has_up))
    def _():
        feat[0] = jnp.zeros(feat.shape[1:], feat.dtype)

    @pl.when(jnp.logical_not(has_down))
    def _():
        feat[rows + 1] = jnp.zeros(feat.shape[1:], feat.dtype)

    vectors_copy.wait()
    rows_wait(0, 3, 0, 0, split)
    for slot in (1, 2, 3):
        norm_part(slot, 0, split)
    space_copies[0].wait()

    @once
    def _():
        begun[...] = taps((1,), ((0, 0, 3), (1, 0, 3)), 0, split)

    space_copies[1].wait()

    @once
    def _():
        space_store(1, begun[...] + taps((1,), ((2, 0, 3),), 0, split), 0, split)

    peers = (
        (band + bands - 1) // bands
        + 1 - (band + 1) // bands
        + (frame + frame_parts - 1) // frame_parts
        + 1 - (frame + 1) // frame_parts
    )
    pl.semaphore_wait(barrier, peers)

    row_send(1, 0, 0, 1)
    to_up = pltpu.make_async_remote_copy(
        features.at[:, 0], feat.at[rows + 1], up_send, halo_recv.at[0],
        device_id={"band": band - 1}, device_id_type=pl.DeviceIdType.MESH,
    )
    to_down = pltpu.make_async_remote_copy(
        features.at[:, rows - 1], feat.at[0], down_send, halo_recv.at[1],
        device_id={"band": band + 1}, device_id_type=pl.DeviceIdType.MESH,
    )
    pl.when(has_up)(to_up.start)
    pl.when(has_down)(to_down.start)

    rows_start(4, rows - 4, 0)
    rows_wait(0, 4, 1, split, frames - split)
    rows_wait(3, 1, 2, 0, split)
    lags_copy.start()

    @once
    def _():
        for slot in (1, 2, 3, 4):
            norm_part(slot, split, frames - split)
        space_part(
            (1, 2), split, frames - split, lambda row: row_send(row, 0, 1, LAGS - 1)
        )

    @once
    def _():
        norm_part(4, 0, split)
        space_part((2,), 0, split)

    row_send(2, 0, 0, 1)
    rows_wait(4, rows - 4, 0)

    @pl.loop(3, last)
    def _(row):
        norm_part(row + 2)
        space_part((row,))
        row_send(row, sum((row >= g).astype(jnp.int32) for g in groups[1:]))

    pl.when(has_up)(to_down.wait_recv)
    pl.when(has_down)(to_up.wait_recv)

    @once
    def _():
        norm_part(0)
        space_part((0,))

    row_send(0, len(groups) - 1)

    @once
    def _():
        norm_part(rows + 1)
        space_part((last,))

    lags_copy.wait()

    @pl.when(has_next)
    def _():
        lag_sums(last)
        for side in range(2):
            columns = pl.ds(side * half, half)
            time_copy(
                partial.at[:, columns],
                earlier.at[last, :, columns],
                len(groups) + side,
            ).start()

    @pl.loop(1, last)
    def _(row):
        for i, start in enumerate(groups):
            count = groups[i + 1] - start if i + 1 < len(groups) else rows - start

            @pl.when(row == start)
            def _():
                time_wait(earlier.at[pl.ds(rows - count, count)], i)

        time_part(row)

    time_part(0)
    totals = own_totals(last)
    for side in range(2):
        columns = slice(side * half, (side + 1) * half)
        time_wait(earlier.at[last, :, pl.ds(side * half, half)], len(groups) + side)
        for f in range(frames):
            total = totals[f][columns]
            if f < LAGS:
                total += earlier[last, f, columns].astype(jnp.float32)
            finish(last, f, total, side * half, half)

    pl.when(has_up)(to_up.wait_send)
    pl.when(has_down)(to_down.wait_send)

    @pl.when(has_next)
    def _():
        pltpu.make_async_copy(earlier, earlier, time_send).wait()


def body(features, *rest):
    frames, rows, cols, channels = features.shape
    bf16 = jnp.bfloat16
    return pl.pallas_call(
        kernel,
        out_shape=jax.ShapeDtypeStruct(features.shape, bf16),
        in_specs=[pl.BlockSpec(memory_space=pltpu.HBM)] * 7,
        out_specs=pl.BlockSpec(memory_space=pltpu.VMEM),
        scratch_shapes=[
            pltpu.VMEM((rows + 2, frames, cols, channels), bf16),
            pltpu.VMEM((rows + 2, frames, cols, 3 * channels), bf16),
            pltpu.VMEM(((frames - LAGS + 1) * cols, channels), jnp.float32),
            pltpu.VMEM((rows, frames, cols, channels), bf16),
            pltpu.VMEM((rows, frames, cols, channels), bf16),
            pltpu.VMEM((rows, LAGS, cols, channels), bf16),
            pltpu.VMEM((LAGS, cols, channels), bf16),
            pltpu.VMEM(rest[0].shape, bf16),
            pltpu.VMEM(rest[3].shape, bf16),
            pltpu.VMEM((4, channels), jnp.float32),
            pltpu.SemaphoreType.DMA((3,)),
            pltpu.SemaphoreType.DMA((3,)),
            pltpu.SemaphoreType.DMA((2,)),
            pltpu.SemaphoreType.DMA((len(group_starts(rows - 1)) + 2,)),
        ],
        compiler_params=pltpu.CompilerParams(
            collective_id=0, has_side_effects=True, vmem_limit_bytes=36 * 1024 * 1024
        ),
    )(*[pltpu.with_memory_space_constraint(x, pltpu.HBM) for x in (features, *rest)])


def solution(mesh):
    return jax.shard_map(
        body,
        mesh=mesh,
        in_specs=(P(("grp", "frame"), "band", None, None), P(), P(), P(), P(), P(), P()),
        out_specs=P(("grp", "frame"), "band", None, None),
        check_vma=False,
    )
```

```python
import functools

import jax
import jax.numpy as jnp
from jax import lax
from jax.experimental import pallas as pl
from jax.experimental.pallas import tpu as pltpu
from jax.sharding import PartitionSpec as P

LAGS = 2


def rms_silu(values, gain):
    mean = jnp.mean(values * values, axis=-1, keepdims=True)
    half = values * lax.rsqrt(mean + 1e-06) * (0.5 * gain)
    return half + half * jnp.tanh(half)


def dot(left, right):
    return jnp.dot(left, right, preferred_element_type=jnp.float32)


def group_starts(last):
    return sorted({min(max(1, start), last - 1) for start in (1, last - 5, last - 1)})


def kernel(
    features, space_kernel, space_gain, space_bias, time_kernel, time_gain, time_bias,
    out,
    feat, normed, begun, hidden, ntime, earlier, partial, wspace, wtime, vectors,
    feat_sem, weight_sem, halo_recv, time_recv,
):
    frames, rows, cols, channels = features.shape
    half = cols // 2
    split = frames - LAGS + 1
    last = rows - 1
    band, bands = lax.axis_index("band"), lax.axis_size("band")
    frame, frame_parts = lax.axis_index("frame"), lax.axis_size("frame")
    has_up, has_down = band > 0, band < bands - 1
    has_prev, has_next = frame > 0, frame < frame_parts - 1
    neighbours = (
        (has_up, {"band": band - 1}),
        (has_down, {"band": band + 1}),
        (has_prev, {"frame": frame - 1}),
        (has_next, {"frame": frame + 1}),
    )

    barrier = pltpu.get_barrier_semaphore()

    def greet(present, device):
        @pl.when(present)
        def _():
            pl.semaphore_signal(
                barrier, inc=1, device_id=device, device_id_type=pl.DeviceIdType.MESH
            )

    def rows_start(first, count, sem, start=0, size=frames, step=None):
        step = step or count
        for f in range(start, start + size):
            for row in range(first, first + count, step):
                pltpu.make_async_copy(
                    features.at[f, pl.ds(row, step)],
                    feat.at[pl.ds(row + 1, step), f],
                    feat_sem.at[sem],
                ).start()

    def rows_wait(first, count, sem, start=0, size=frames):
        block = feat.at[pl.ds(first + 1, count), pl.ds(start, size)]
        pltpu.make_async_copy(block, block, feat_sem.at[sem]).wait()

    vector_copies = [
        pltpu.make_async_copy(vector, vectors.at[i], weight_sem.at[0])
        for i, vector in enumerate((space_gain, space_bias, time_gain, time_bias))
    ]
    vectors_copy = pltpu.make_async_copy(vectors, vectors, weight_sem.at[0])
    space_copies = [
        pltpu.make_async_copy(
            space_kernel.at[pl.ds(start, count)],
            wspace.at[pl.ds(start, count)],
            weight_sem.at[sem],
        )
        for start, count, sem in ((0, 4, 1), (4, 5, 2))
    ]
    lags_copy = pltpu.make_async_copy(time_kernel, wtime, feat_sem.at[2])
    rows_start(0, 3, 0, 0, split, 1)
    for copy in vector_copies:
        copy.start()
    greet(*neighbours[2])
    for copy in space_copies:
        copy.start()
    for i in (0, 1, 3):
        greet(*neighbours[i])
    rows_start(0, 4, 1, split, frames - split)
    rows_start(3, 1, 2, 0, split)

    time_send, up_send, down_send = (weight_sem.at[i] for i in range(3))
    groups = group_starts(last)

    def time_copy(source, target, sem):
        return pltpu.make_async_remote_copy(
            source,
            target,
            time_send,
            time_recv.at[sem],
            device_id={"frame": frame + 1},
            device_id_type=pl.DeviceIdType.MESH,
        )

    def row_send(row, sem, start=0, count=LAGS):
        source = ntime.at[row, pl.ds(frames - LAGS + start, count)]
        target = earlier.at[row, pl.ds(start, count)]
        pl.when(has_next)(time_copy(source, target, sem).start)

    def time_wait(block, sem):
        pl.when(has_prev)(
            pltpu.make_async_copy(block, block, time_recv.at[sem]).wait
        )

    def vector(i):
        return vectors[i].reshape(1, channels)

    def norm_part(slot, start=0, count=frames):
        size = count * cols
        values = feat[slot, start : start + count]
        result = rms_silu(values.reshape(size, channels).astype(jnp.float32), vector(0))
        column = lax.rem(lax.broadcasted_iota(jnp.int32, (size, channels), 0), cols)
        before = jnp.where(column == 0, 0.0, pltpu.roll(result, 1, 0))
        after = jnp.where(column == cols - 1, 0.0, pltpu.roll(result, size - 1, 0))
        for i, piece in enumerate((before, result, after)):
            normed[
                slot, start : start + count, :, i * channels : (i + 1) * channels
            ] = piece.astype(jnp.bfloat16).reshape(count, cols, channels)

    def taps(block, chosen, start, count):
        total = None
        for i, low, high in chosen:
            columns = slice(low * channels, high * channels)
            parts = [
                normed[row + i, start : start + count, :, columns]
                for row in block
            ]
            parts = [part.reshape(-1, (high - low) * channels) for part in parts]
            left = parts[0] if len(parts) == 1 else jnp.concatenate(parts, 0)
            term = dot(left, wspace[3 * i + low : 3 * i + high].reshape(-1, channels))
            total = term if total is None else total + term
        return total

    def space_store(row, total, start, count):
        shape = (count, cols, channels)
        where = slice(start, start + count)
        centre = feat[row + 1, where].reshape(-1, channels).astype(jnp.float32)
        kept = (centre + total + vector(1)).astype(jnp.bfloat16)
        hidden[row, where] = kept.reshape(shape)
        after = rms_silu(kept.astype(jnp.float32), vector(2))
        ntime[row, where] = after.astype(jnp.bfloat16).reshape(shape)

    def space_part(block, start=0, count=frames, stored=lambda row: None):
        total = taps(block, ((0, 0, 3), (1, 0, 3), (2, 0, 3)), start, count)
        size = count * cols
        for i, row in enumerate(block):
            space_store(row, total[i * size : (i + 1) * size], start, count)
            stored(row)

    def once(step):
        pl.loop(0, 1 + band // bands)(lambda _: step())

    def own_totals(row):
        own = ntime[row]
        totals = [
            dot(own.reshape(-1, channels), wtime[0]).reshape(own.shape)[f]
            for f in range(frames)
        ]
        for lag in range(1, min(LAGS, frames - 1) + 1):
            term = dot(own[: frames - lag].reshape(-1, channels), wtime[lag])
            for f in range(lag, frames):
                totals[f] += term[(f - lag) * cols : (f - lag + 1) * cols]
        return totals

    def finish(row, f, total, left=0, width=cols):
        columns = slice(left, left + width)
        temporal = total.astype(jnp.bfloat16).astype(jnp.float32)
        kept = hidden[row, f, columns].astype(jnp.float32)
        out[f, row, columns] = (kept + temporal + vector(3)).astype(jnp.bfloat16)

    def time_part(row):
        totals = own_totals(row)
        for lag in range(1, LAGS + 1):
            past = earlier[row, LAGS - lag :]
            term = dot(past.reshape(-1, channels), wtime[lag])
            for f in range(lag):
                totals[f] += term[f * cols : (f + 1) * cols]
        for f in range(frames):
            finish(row, f, totals[f])

    def lag_sums(row):
        for f in range(LAGS):
            total = None
            for lag in range(f + 1, LAGS + 1):
                term = dot(ntime[row, frames - lag + f], wtime[lag])
                total = term if total is None else total + term
            partial[f] = total.astype(jnp.bfloat16)

    @pl.when(jnp.logical_not(has_prev))
    def _():
        earlier[...] = jnp.zeros_like(earlier)

    @pl.when(jnp.logical_not(has_up))
    def _():
        feat[0] = jnp.zeros(feat.shape[1:], feat.dtype)

    @pl.when(jnp.logical_not(has_down))
    def _():
        feat[rows + 1] = jnp.zeros(feat.shape[1:], feat.dtype)

    vectors_copy.wait()
    rows_wait(0, 3, 0, 0, split)
    for slot in (1, 2, 3):
        norm_part(slot, 0, split)
    space_copies[0].wait()

    @once
    def _():
        begun[...] = taps((1,), ((0, 0, 3), (1, 0, 1)), 0, split)

    space_copies[1].wait()

    @once
    def _():
        rest = taps((1,), ((1, 1, 3), (2, 0, 3)), 0, split)
        space_store(1, begun[...] + rest, 0, split)

    peers = (
        (band + bands - 1) // bands
        + 1 - (band + 1) // bands
        + (frame + frame_parts - 1) // frame_parts
        + 1 - (frame + 1) // frame_parts
    )
    pl.semaphore_wait(barrier, peers)

    row_send(1, 0, 0, 1)
    to_up = pltpu.make_async_remote_copy(
        features.at[:, 0], feat.at[rows + 1], up_send, halo_recv.at[0],
        device_id={"band": band - 1}, device_id_type=pl.DeviceIdType.MESH,
    )
    to_down = pltpu.make_async_remote_copy(
        features.at[:, rows - 1], feat.at[0], down_send, halo_recv.at[1],
        device_id={"band": band + 1}, device_id_type=pl.DeviceIdType.MESH,
    )
    pl.when(has_up)(to_up.start)
    pl.when(has_down)(to_down.start)

    rows_start(4, rows - 4, 0)
    rows_wait(0, 4, 1, split, frames - split)
    rows_wait(3, 1, 2, 0, split)
    lags_copy.start()

    @once
    def _():
        for slot in (1, 2, 3, 4):
            norm_part(slot, split, frames - split)
        space_part(
            (1, 2), split, frames - split, lambda row: row_send(row, 0, 1, LAGS - 1)
        )

    @once
    def _():
        norm_part(4, 0, split)
        space_part((2,), 0, split)

    row_send(2, 0, 0, 1)
    rows_wait(4, rows - 4, 0)

    @pl.loop(3, last)
    def _(row):
        norm_part(row + 2)
        space_part((row,))
        row_send(row, sum((row >= g).astype(jnp.int32) for g in groups[1:]))

    pl.when(has_up)(to_down.wait_recv)
    pl.when(has_down)(to_up.wait_recv)

    @once
    def _():
        norm_part(0)
        space_part((0,))

    row_send(0, len(groups) - 1)

    @once
    def _():
        norm_part(rows + 1)
        space_part((last,))

    lags_copy.wait()

    @pl.when(has_next)
    def _():
        lag_sums(last)
        for side in range(2):
            columns = pl.ds(side * half, half)
            time_copy(
                partial.at[:, columns],
                earlier.at[last, :, columns],
                len(groups) + side,
            ).start()

    @pl.loop(1, last)
    def _(row):
        for i, start in enumerate(groups):
            count = groups[i + 1] - start if i + 1 < len(groups) else rows - start

            @pl.when(row == start)
            def _():
                time_wait(earlier.at[pl.ds(rows - count, count)], i)

        time_part(row)

    time_part(0)
    totals = own_totals(last)
    for side in range(2):
        columns = slice(side * half, (side + 1) * half)
        time_wait(earlier.at[last, :, pl.ds(side * half, half)], len(groups) + side)
        for f in range(frames):
            total = totals[f][columns]
            if f < LAGS:
                total += earlier[last, f, columns].astype(jnp.float32)
            finish(last, f, total, side * half, half)

    pl.when(has_up)(to_up.wait_send)
    pl.when(has_down)(to_down.wait_send)

    @pl.when(has_next)
    def _():
        pltpu.make_async_copy(earlier, earlier, time_send).wait()


def body(features, *rest):
    frames, rows, cols, channels = features.shape
    bf16 = jnp.bfloat16
    rest = (rest[0].reshape(-1, channels, channels), *rest[1:])
    return pl.pallas_call(
        kernel,
        out_shape=jax.ShapeDtypeStruct(features.shape, bf16),
        in_specs=[pl.BlockSpec(memory_space=pltpu.HBM)] * 7,
        out_specs=pl.BlockSpec(memory_space=pltpu.VMEM),
        scratch_shapes=[
            pltpu.VMEM((rows + 2, frames, cols, channels), bf16),
            pltpu.VMEM((rows + 2, frames, cols, 3 * channels), bf16),
            pltpu.VMEM(((frames - LAGS + 1) * cols, channels), jnp.float32),
            pltpu.VMEM((rows, frames, cols, channels), bf16),
            pltpu.VMEM((rows, frames, cols, channels), bf16),
            pltpu.VMEM((rows, LAGS, cols, channels), bf16),
            pltpu.VMEM((LAGS, cols, channels), bf16),
            pltpu.VMEM(rest[0].shape, bf16),
            pltpu.VMEM(rest[3].shape, bf16),
            pltpu.VMEM((4, channels), jnp.float32),
            pltpu.SemaphoreType.DMA((3,)),
            pltpu.SemaphoreType.DMA((3,)),
            pltpu.SemaphoreType.DMA((2,)),
            pltpu.SemaphoreType.DMA((len(group_starts(rows - 1)) + 2,)),
        ],
        compiler_params=pltpu.CompilerParams(
            collective_id=0, has_side_effects=True, vmem_limit_bytes=36 * 1024 * 1024
        ),
    )(*[pltpu.with_memory_space_constraint(x, pltpu.HBM) for x in (features, *rest)])


def solution(mesh):
    return jax.shard_map(
        body,
        mesh=mesh,
        in_specs=(P(("grp", "frame"), "band", None, None), P(), P(), P(), P(), P(), P()),
        out_specs=P(("grp", "frame"), "band", None, None),
        check_vma=False,
    )
```

```python
import functools

import jax
import jax.numpy as jnp
from jax import lax
from jax.experimental import pallas as pl
from jax.experimental.pallas import tpu as pltpu
from jax.sharding import PartitionSpec as P

LAGS = 2


def rms_silu(values, gain):
    mean = jnp.mean(values * values, axis=-1, keepdims=True)
    half = values * lax.rsqrt(mean + 1e-06) * (0.5 * gain)
    return half + half * jnp.tanh(half)


def dot(left, right):
    return jnp.dot(left, right, preferred_element_type=jnp.float32)


def group_starts(last):
    return sorted({min(max(1, start), last - 1) for start in (1, last - 5, last - 1)})


def kernel(
    features, space_kernel, space_gain, space_bias, time_kernel, time_gain, time_bias,
    out,
    feat, normed, begun, hidden, ntime, earlier, partial, wspace, wtime, vectors,
    feat_sem, weight_sem, halo_recv, time_recv,
):
    frames, rows, cols, channels = features.shape
    half = cols // 2
    split = frames - LAGS + 1
    last = rows - 1
    band, bands = lax.axis_index("band"), lax.axis_size("band")
    frame, frame_parts = lax.axis_index("frame"), lax.axis_size("frame")
    has_up, has_down = band > 0, band < bands - 1
    has_prev, has_next = frame > 0, frame < frame_parts - 1
    neighbours = (
        (has_up, {"band": band - 1}),
        (has_down, {"band": band + 1}),
        (has_prev, {"frame": frame - 1}),
        (has_next, {"frame": frame + 1}),
    )

    barrier = pltpu.get_barrier_semaphore()

    def greet(present, device):
        @pl.when(present)
        def _():
            pl.semaphore_signal(
                barrier, inc=1, device_id=device, device_id_type=pl.DeviceIdType.MESH
            )

    def rows_start(first, count, sem, start=0, size=frames, step=None, width=cols):
        step = step or count
        for f in range(start, start + size):
            for row in range(first, first + count, step):
                for left in range(0, cols, width):
                    columns = pl.ds(left, width)
                    pltpu.make_async_copy(
                        features.at[f, pl.ds(row, step), columns],
                        feat.at[pl.ds(row + 1, step), f, columns],
                        feat_sem.at[sem],
                    ).start()

    def rows_wait(first, count, sem, start=0, size=frames):
        block = feat.at[pl.ds(first + 1, count), pl.ds(start, size)]
        pltpu.make_async_copy(block, block, feat_sem.at[sem]).wait()

    vector_copies = [
        pltpu.make_async_copy(vector, vectors.at[i], weight_sem.at[0])
        for i, vector in enumerate((space_gain, space_bias, time_gain, time_bias))
    ]
    vectors_copy = pltpu.make_async_copy(vectors, vectors, weight_sem.at[0])
    space_copies = [
        pltpu.make_async_copy(
            space_kernel.at[pl.ds(start, count)],
            wspace.at[pl.ds(start, count)],
            weight_sem.at[sem],
        )
        for start, count, sem in ((0, 3, 1), (3, 6, 2))
    ]
    lags_copy = pltpu.make_async_copy(time_kernel, wtime, feat_sem.at[2])
    rows_start(0, 3, 0, 0, split, 1, half)
    for copy in vector_copies:
        copy.start()
    greet(*neighbours[2])
    for copy in space_copies:
        copy.start()
    for i in (0, 1, 3):
        greet(*neighbours[i])
    rows_start(0, 4, 1, split, frames - split)
    rows_start(3, 1, 2, 0, split)

    time_send, up_send, down_send = (weight_sem.at[i] for i in range(3))
    groups = group_starts(last)

    def time_copy(source, target, sem):
        return pltpu.make_async_remote_copy(
            source,
            target,
            time_send,
            time_recv.at[sem],
            device_id={"frame": frame + 1},
            device_id_type=pl.DeviceIdType.MESH,
        )

    def row_send(row, sem, start=0, count=LAGS):
        source = ntime.at[row, pl.ds(frames - LAGS + start, count)]
        target = earlier.at[row, pl.ds(start, count)]
        pl.when(has_next)(time_copy(source, target, sem).start)

    def time_wait(block, sem):
        pl.when(has_prev)(
            pltpu.make_async_copy(block, block, time_recv.at[sem]).wait
        )

    def vector(i):
        return vectors[i].reshape(1, channels)

    def norm_part(slot, start=0, count=frames):
        size = count * cols
        values = feat[slot, start : start + count]
        result = rms_silu(values.reshape(size, channels).astype(jnp.float32), vector(0))
        column = lax.rem(lax.broadcasted_iota(jnp.int32, (size, channels), 0), cols)
        before = jnp.where(column == 0, 0.0, pltpu.roll(result, 1, 0))
        after = jnp.where(column == cols - 1, 0.0, pltpu.roll(result, size - 1, 0))
        for i, piece in enumerate((before, result, after)):
            normed[
                slot, start : start + count, :, i * channels : (i + 1) * channels
            ] = piece.astype(jnp.bfloat16).reshape(count, cols, channels)

    def taps(block, chosen, start, count):
        total = None
        for i, low, high in chosen:
            columns = slice(low * channels, high * channels)
            parts = [
                normed[row + i, start : start + count, :, columns]
                for row in block
            ]
            parts = [part.reshape(-1, (high - low) * channels) for part in parts]
            left = parts[0] if len(parts) == 1 else jnp.concatenate(parts, 0)
            term = dot(left, wspace[3 * i + low : 3 * i + high].reshape(-1, channels))
            total = term if total is None else total + term
        return total

    def space_store(row, total, start, count):
        shape = (count, cols, channels)
        where = slice(start, start + count)
        centre = feat[row + 1, where].reshape(-1, channels).astype(jnp.float32)
        kept = (centre + total + vector(1)).astype(jnp.bfloat16)
        hidden[row, where] = kept.reshape(shape)
        after = rms_silu(kept.astype(jnp.float32), vector(2))
        ntime[row, where] = after.astype(jnp.bfloat16).reshape(shape)

    def space_part(block, start=0, count=frames, stored=lambda row: None):
        total = taps(block, ((0, 0, 3), (1, 0, 3), (2, 0, 3)), start, count)
        size = count * cols
        for i, row in enumerate(block):
            space_store(row, total[i * size : (i + 1) * size], start, count)
            stored(row)

    def once(step):
        pl.loop(0, 1 + band // bands)(lambda _: step())

    def own_totals(row):
        own = ntime[row]
        totals = [
            dot(own.reshape(-1, channels), wtime[0]).reshape(own.shape)[f]
            for f in range(frames)
        ]
        for lag in range(1, min(LAGS, frames - 1) + 1):
            term = dot(own[: frames - lag].reshape(-1, channels), wtime[lag])
            for f in range(lag, frames):
                totals[f] += term[(f - lag) * cols : (f - lag + 1) * cols]
        return totals

    def finish(row, f, total, left=0, width=cols):
        columns = slice(left, left + width)
        temporal = total.astype(jnp.bfloat16).astype(jnp.float32)
        kept = hidden[row, f, columns].astype(jnp.float32)
        out[f, row, columns] = (kept + temporal + vector(3)).astype(jnp.bfloat16)

    def time_part(row):
        totals = own_totals(row)
        for lag in range(1, LAGS + 1):
            past = earlier[row, LAGS - lag :]
            term = dot(past.reshape(-1, channels), wtime[lag])
            for f in range(lag):
                totals[f] += term[f * cols : (f + 1) * cols]
        for f in range(frames):
            finish(row, f, totals[f])

    def lag_sums(row):
        for f in range(LAGS):
            total = None
            for lag in range(f + 1, LAGS + 1):
                term = dot(ntime[row, frames - lag + f], wtime[lag])
                total = term if total is None else total + term
            partial[f] = total.astype(jnp.bfloat16)

    @pl.when(jnp.logical_not(has_prev))
    def _():
        earlier[...] = jnp.zeros_like(earlier)

    @pl.when(jnp.logical_not(has_up))
    def _():
        feat[0] = jnp.zeros(feat.shape[1:], feat.dtype)

    @pl.when(jnp.logical_not(has_down))
    def _():
        feat[rows + 1] = jnp.zeros(feat.shape[1:], feat.dtype)

    vectors_copy.wait()
    rows_wait(0, 3, 0, 0, split)
    for slot in (1, 2, 3):
        norm_part(slot, 0, split)
    space_copies[0].wait()

    @once
    def _():
        begun[...] = taps((1,), ((0, 0, 3),), 0, split)

    space_copies[1].wait()

    @once
    def _():
        rest = taps((1,), ((1, 0, 3), (2, 0, 3)), 0, split)
        space_store(1, begun[...] + rest, 0, split)

    peers = (
        (band + bands - 1) // bands
        + 1 - (band + 1) // bands
        + (frame + frame_parts - 1) // frame_parts
        + 1 - (frame + 1) // frame_parts
    )
    pl.semaphore_wait(barrier, peers)

    row_send(1, 0, 0, 1)
    to_up = pltpu.make_async_remote_copy(
        features.at[:, 0], feat.at[rows + 1], up_send, halo_recv.at[0],
        device_id={"band": band - 1}, device_id_type=pl.DeviceIdType.MESH,
    )
    to_down = pltpu.make_async_remote_copy(
        features.at[:, rows - 1], feat.at[0], down_send, halo_recv.at[1],
        device_id={"band": band + 1}, device_id_type=pl.DeviceIdType.MESH,
    )
    pl.when(has_up)(to_up.start)
    pl.when(has_down)(to_down.start)

    rows_start(4, rows - 4, 0)
    rows_wait(0, 4, 1, split, frames - split)
    rows_wait(3, 1, 2, 0, split)
    lags_copy.start()

    @once
    def _():
        for slot in (1, 2, 3, 4):
            norm_part(slot, split, frames - split)
        space_part(
            (1, 2), split, frames - split, lambda row: row_send(row, 0, 1, LAGS - 1)
        )

    @once
    def _():
        norm_part(4, 0, split)
        space_part((2,), 0, split)

    row_send(2, 0, 0, 1)
    rows_wait(4, rows - 4, 0)

    @pl.loop(3, last)
    def _(row):
        norm_part(row + 2)
        space_part((row,))
        row_send(row, sum((row >= g).astype(jnp.int32) for g in groups[1:]))

    pl.when(has_up)(to_down.wait_recv)
    pl.when(has_down)(to_up.wait_recv)

    @once
    def _():
        norm_part(0)
        space_part((0,))

    row_send(0, len(groups) - 1)

    @once
    def _():
        norm_part(rows + 1)
        space_part((last,))

    lags_copy.wait()

    @pl.when(has_next)
    def _():
        lag_sums(last)
        for side in range(2):
            columns = pl.ds(side * half, half)
            time_copy(
                partial.at[:, columns],
                earlier.at[last, :, columns],
                len(groups) + side,
            ).start()

    @pl.loop(1, last)
    def _(row):
        for i, start in enumerate(groups):
            count = groups[i + 1] - start if i + 1 < len(groups) else rows - start

            @pl.when(row == start)
            def _():
                time_wait(earlier.at[pl.ds(rows - count, count)], i)

        time_part(row)

    time_part(0)
    totals = own_totals(last)
    for side in range(2):
        columns = slice(side * half, (side + 1) * half)
        time_wait(earlier.at[last, :, pl.ds(side * half, half)], len(groups) + side)
        for f in range(frames):
            total = totals[f][columns]
            if f < LAGS:
                total += earlier[last, f, columns].astype(jnp.float32)
            finish(last, f, total, side * half, half)

    pl.when(has_up)(to_up.wait_send)
    pl.when(has_down)(to_down.wait_send)

    @pl.when(has_next)
    def _():
        pltpu.make_async_copy(earlier, earlier, time_send).wait()


def body(features, *rest):
    frames, rows, cols, channels = features.shape
    bf16 = jnp.bfloat16
    rest = (rest[0].reshape(-1, channels, channels), *rest[1:])
    return pl.pallas_call(
        kernel,
        out_shape=jax.ShapeDtypeStruct(features.shape, bf16),
        in_specs=[pl.BlockSpec(memory_space=pltpu.HBM)] * 7,
        out_specs=pl.BlockSpec(memory_space=pltpu.VMEM),
        scratch_shapes=[
            pltpu.VMEM((rows + 2, frames, cols, channels), bf16),
            pltpu.VMEM((rows + 2, frames, cols, 3 * channels), bf16),
            pltpu.VMEM(((frames - LAGS + 1) * cols, channels), jnp.float32),
            pltpu.VMEM((rows, frames, cols, channels), bf16),
            pltpu.VMEM((rows, frames, cols, channels), bf16),
            pltpu.VMEM((rows, LAGS, cols, channels), bf16),
            pltpu.VMEM((LAGS, cols, channels), bf16),
            pltpu.VMEM(rest[0].shape, bf16),
            pltpu.VMEM(rest[3].shape, bf16),
            pltpu.VMEM((4, channels), jnp.float32),
            pltpu.SemaphoreType.DMA((3,)),
            pltpu.SemaphoreType.DMA((3,)),
            pltpu.SemaphoreType.DMA((2,)),
            pltpu.SemaphoreType.DMA((len(group_starts(rows - 1)) + 2,)),
        ],
        compiler_params=pltpu.CompilerParams(
            collective_id=0, has_side_effects=True, vmem_limit_bytes=36 * 1024 * 1024
        ),
    )(*[pltpu.with_memory_space_constraint(x, pltpu.HBM) for x in (features, *rest)])


def solution(mesh):
    return jax.shard_map(
        body,
        mesh=mesh,
        in_specs=(P(("grp", "frame"), "band", None, None), P(), P(), P(), P(), P(), P()),
        out_specs=P(("grp", "frame"), "band", None, None),
        check_vma=False,
    )
```

```python
import functools

import jax
import jax.numpy as jnp
from jax import lax
from jax.experimental import pallas as pl
from jax.experimental.pallas import tpu as pltpu
from jax.sharding import PartitionSpec as P

LAGS = 2


def rms_silu(values, gain):
    mean = jnp.mean(values * values, axis=-1, keepdims=True)
    half = values * lax.rsqrt(mean + 1e-06) * (0.5 * gain)
    return half + half * jnp.tanh(half)


def dot(left, right):
    return jnp.dot(left, right, preferred_element_type=jnp.float32)


def group_starts(last):
    return sorted({min(max(1, start), last - 1) for start in (1, last - 5, last - 1)})


def kernel(
    features, space_kernel, space_gain, space_bias, time_kernel, time_gain, time_bias,
    out,
    feat, normed, begun, hidden, ntime, earlier, partial, wspace, wtime, vectors,
    feat_sem, weight_sem, halo_recv, time_recv,
):
    frames, rows, cols, channels = features.shape
    half = cols // 2
    split = frames - LAGS + 1
    last = rows - 1
    band, bands = lax.axis_index("band"), lax.axis_size("band")
    frame, frame_parts = lax.axis_index("frame"), lax.axis_size("frame")
    has_up, has_down = band > 0, band < bands - 1
    has_prev, has_next = frame > 0, frame < frame_parts - 1
    neighbours = (
        (has_up, {"band": band - 1}),
        (has_down, {"band": band + 1}),
        (has_prev, {"frame": frame - 1}),
        (has_next, {"frame": frame + 1}),
    )

    barrier = pltpu.get_barrier_semaphore()

    def greet(present, device):
        @pl.when(present)
        def _():
            pl.semaphore_signal(
                barrier, inc=1, device_id=device, device_id_type=pl.DeviceIdType.MESH
            )

    def rows_start(first, count, sem, start=0, size=frames, step=None, width=cols):
        step = step or count
        for f in range(start, start + size):
            for row in range(first, first + count, step):
                for left in range(0, cols, width):
                    columns = pl.ds(left, width)
                    pltpu.make_async_copy(
                        features.at[f, pl.ds(row, step), columns],
                        feat.at[pl.ds(row + 1, step), f, columns],
                        feat_sem.at[sem],
                    ).start()

    def rows_wait(first, count, sem, start=0, size=frames):
        block = feat.at[pl.ds(first + 1, count), pl.ds(start, size)]
        pltpu.make_async_copy(block, block, feat_sem.at[sem]).wait()

    vector_copies = [
        pltpu.make_async_copy(vector, vectors.at[i], weight_sem.at[0])
        for i, vector in enumerate((space_gain, space_bias, time_gain, time_bias))
    ]
    vectors_copy = pltpu.make_async_copy(vectors, vectors, weight_sem.at[0])
    space_copies = [
        pltpu.make_async_copy(
            space_kernel.at[pl.ds(start, count)],
            wspace.at[pl.ds(start, count)],
            weight_sem.at[sem],
        )
        for start, count, sem in ((0, 3, 1), (3, 6, 2))
    ]
    lags_copy = pltpu.make_async_copy(time_kernel, wtime, feat_sem.at[1])
    greet(*neighbours[2])
    rows_start(0, 3, 0, 0, split, 1, half)
    for copy in vector_copies:
        copy.start()
    greet(*neighbours[3])
    for copy in space_copies:
        copy.start()
    for i in (0, 1):
        greet(*neighbours[i])
    rows_start(0, 4, 1, split, frames - split)
    rows_start(3, 1, 1, 0, split)

    time_send, halo_send = weight_sem.at[0], weight_sem.at[1]
    groups = group_starts(last)

    def time_copy(source, target, sem):
        return pltpu.make_async_remote_copy(
            source,
            target,
            time_send,
            time_recv.at[sem],
            device_id={"frame": frame + 1},
            device_id_type=pl.DeviceIdType.MESH,
        )

    def row_send(row, sem, start=0, count=LAGS):
        source = ntime.at[row, pl.ds(frames - LAGS + start, count)]
        target = earlier.at[row, pl.ds(start, count)]
        pl.when(has_next)(time_copy(source, target, sem).start)

    def halo_wait(sem):
        for count, present in ((2, has_up & has_down), (1, has_up != has_down)):
            block = feat.at[pl.ds(0, count)]
            pl.when(present)(pltpu.make_async_copy(block, block, sem).wait)

    def time_wait(block, sem):
        pl.when(has_prev)(
            pltpu.make_async_copy(block, block, time_recv.at[sem]).wait
        )

    def vector(i):
        return vectors[i].reshape(1, channels)

    def norm_part(slot, start=0, count=frames):
        size = count * cols
        values = feat[slot, start : start + count]
        result = rms_silu(values.reshape(size, channels).astype(jnp.float32), vector(0))
        column = lax.rem(lax.broadcasted_iota(jnp.int32, (size, channels), 0), cols)
        before = jnp.where(column == 0, 0.0, pltpu.roll(result, 1, 0))
        after = jnp.where(column == cols - 1, 0.0, pltpu.roll(result, size - 1, 0))
        for i, piece in enumerate((before, result, after)):
            normed[
                slot, start : start + count, :, i * channels : (i + 1) * channels
            ] = piece.astype(jnp.bfloat16).reshape(count, cols, channels)

    def taps(block, chosen, start, count):
        total = None
        for i, low, high in chosen:
            columns = slice(low * channels, high * channels)
            parts = [
                normed[row + i, start : start + count, :, columns]
                for row in block
            ]
            parts = [part.reshape(-1, (high - low) * channels) for part in parts]
            left = parts[0] if len(parts) == 1 else jnp.concatenate(parts, 0)
            term = dot(left, wspace[3 * i + low : 3 * i + high].reshape(-1, channels))
            total = term if total is None else total + term
        return total

    def space_store(row, total, start, count):
        shape = (count, cols, channels)
        where = slice(start, start + count)
        centre = feat[row + 1, where].reshape(-1, channels).astype(jnp.float32)
        kept = (centre + total + vector(1)).astype(jnp.bfloat16)
        hidden[row, where] = kept.reshape(shape)
        after = rms_silu(kept.astype(jnp.float32), vector(2))
        ntime[row, where] = after.astype(jnp.bfloat16).reshape(shape)

    def space_part(block, start=0, count=frames, stored=lambda row: None):
        total = taps(block, ((0, 0, 3), (1, 0, 3), (2, 0, 3)), start, count)
        size = count * cols
        for i, row in enumerate(block):
            space_store(row, total[i * size : (i + 1) * size], start, count)
            stored(row)

    def once(step):
        pl.loop(0, 1 + band // bands)(lambda _: step())

    def own_totals(row):
        own = ntime[row]
        totals = [
            dot(own.reshape(-1, channels), wtime[0]).reshape(own.shape)[f]
            for f in range(frames)
        ]
        for lag in range(1, min(LAGS, frames - 1) + 1):
            term = dot(own[: frames - lag].reshape(-1, channels), wtime[lag])
            for f in range(lag, frames):
                totals[f] += term[(f - lag) * cols : (f - lag + 1) * cols]
        return totals

    def finish(row, f, total, left=0, width=cols):
        columns = slice(left, left + width)
        temporal = total.astype(jnp.bfloat16).astype(jnp.float32)
        kept = hidden[row, f, columns].astype(jnp.float32)
        out[f, row, columns] = (kept + temporal + vector(3)).astype(jnp.bfloat16)

    def time_part(row):
        totals = own_totals(row)
        for lag in range(1, LAGS + 1):
            past = earlier[row, LAGS - lag :]
            term = dot(past.reshape(-1, channels), wtime[lag])
            for f in range(lag):
                totals[f] += term[f * cols : (f + 1) * cols]
        for f in range(frames):
            finish(row, f, totals[f])

    def lag_sums(row):
        for f in range(LAGS):
            total = None
            for lag in range(f + 1, LAGS + 1):
                term = dot(ntime[row, frames - lag + f], wtime[lag])
                total = term if total is None else total + term
            partial[f] = total.astype(jnp.bfloat16)

    @pl.when(jnp.logical_not(has_prev))
    def _():
        earlier[...] = jnp.zeros_like(earlier)

    @pl.when(jnp.logical_not(has_up))
    def _():
        feat[0] = jnp.zeros(feat.shape[1:], feat.dtype)

    @pl.when(jnp.logical_not(has_down))
    def _():
        feat[rows + 1] = jnp.zeros(feat.shape[1:], feat.dtype)

    vectors_copy.wait()
    rows_wait(0, 3, 0, 0, split)
    for slot in (1, 2, 3):
        norm_part(slot, 0, split)
    space_copies[0].wait()

    @once
    def _():
        begun[...] = taps((1,), ((0, 0, 3),), 0, split)

    space_copies[1].wait()

    @once
    def _():
        rest = taps((1,), ((1, 0, 3), (2, 0, 3)), 0, split)
        space_store(1, begun[...] + rest, 0, split)

    peers = (
        (band + bands - 1) // bands
        + 1 - (band + 1) // bands
        + (frame + frame_parts - 1) // frame_parts
        + 1 - (frame + 1) // frame_parts
    )
    pl.semaphore_wait(barrier, peers)

    row_send(1, 0, 0, 1)
    to_up = pltpu.make_async_remote_copy(
        features.at[:, 0], feat.at[rows + 1], halo_send, halo_recv.at[0],
        device_id={"band": band - 1}, device_id_type=pl.DeviceIdType.MESH,
    )
    to_down = pltpu.make_async_remote_copy(
        features.at[:, rows - 1], feat.at[0], halo_send, halo_recv.at[0],
        device_id={"band": band + 1}, device_id_type=pl.DeviceIdType.MESH,
    )
    pl.when(has_up)(to_up.start)
    pl.when(has_down)(to_down.start)

    rows_start(4, rows - 4, 0)
    rows_wait(0, 4 * (frames - split) + split, 1, 0, 1)
    lags_copy.start()

    @once
    def _():
        for slot in (1, 2, 3, 4):
            norm_part(slot, split, frames - split)
        space_part(
            (1, 2), split, frames - split, lambda row: row_send(row, 0, 1, LAGS - 1)
        )

    @once
    def _():
        norm_part(4, 0, split)
        space_part((2,), 0, split)

    row_send(2, 0, 0, 1)
    rows_wait(4, rows - 4, 0)

    @pl.loop(3, last)
    def _(row):
        norm_part(row + 2)
        space_part((row,))
        row_send(row, sum((row >= g).astype(jnp.int32) for g in groups[1:]))

    halo_wait(halo_recv.at[0])

    @once
    def _():
        norm_part(0)
        space_part((0,))

    row_send(0, len(groups) - 1)

    @once
    def _():
        norm_part(rows + 1)
        space_part((last,))

    lags_copy.wait()

    @pl.when(has_next)
    def _():
        lag_sums(last)
        for side in range(2):
            columns = pl.ds(side * half, half)
            time_copy(
                partial.at[:, columns],
                earlier.at[last, :, columns],
                len(groups) + side,
            ).start()

    @pl.loop(1, last)
    def _(row):
        for i, start in enumerate(groups):
            count = groups[i + 1] - start if i + 1 < len(groups) else rows - start

            @pl.when(row == start)
            def _():
                time_wait(earlier.at[pl.ds(rows - count, count)], i)

        time_part(row)

    time_part(0)
    totals = own_totals(last)
    for side in range(2):
        columns = slice(side * half, (side + 1) * half)
        time_wait(earlier.at[last, :, pl.ds(side * half, half)], len(groups) + side)
        for f in range(frames):
            total = totals[f][columns]
            if f < LAGS:
                total += earlier[last, f, columns].astype(jnp.float32)
            finish(last, f, total, side * half, half)

    halo_wait(halo_send)

    @pl.when(has_next)
    def _():
        pltpu.make_async_copy(earlier, earlier, time_send).wait()


def body(features, *rest):
    frames, rows, cols, channels = features.shape
    bf16 = jnp.bfloat16
    rest = (rest[0].reshape(-1, channels, channels), *rest[1:])
    return pl.pallas_call(
        kernel,
        out_shape=jax.ShapeDtypeStruct(features.shape, bf16),
        in_specs=[pl.BlockSpec(memory_space=pltpu.HBM)] * 7,
        out_specs=pl.BlockSpec(memory_space=pltpu.VMEM),
        scratch_shapes=[
            pltpu.VMEM((rows + 2, frames, cols, channels), bf16),
            pltpu.VMEM((rows + 2, frames, cols, 3 * channels), bf16),
            pltpu.VMEM(((frames - LAGS + 1) * cols, channels), jnp.float32),
            pltpu.VMEM((rows, frames, cols, channels), bf16),
            pltpu.VMEM((rows, frames, cols, channels), bf16),
            pltpu.VMEM((rows, LAGS, cols, channels), bf16),
            pltpu.VMEM((LAGS, cols, channels), bf16),
            pltpu.VMEM(rest[0].shape, bf16),
            pltpu.VMEM(rest[3].shape, bf16),
            pltpu.VMEM((4, channels), jnp.float32),
            pltpu.SemaphoreType.DMA((2,)),
            pltpu.SemaphoreType.DMA((3,)),
            pltpu.SemaphoreType.DMA((1,)),
            pltpu.SemaphoreType.DMA((len(group_starts(rows - 1)) + 2,)),
        ],
        compiler_params=pltpu.CompilerParams(
            collective_id=0, has_side_effects=True, vmem_limit_bytes=36 * 1024 * 1024
        ),
    )(*[pltpu.with_memory_space_constraint(x, pltpu.HBM) for x in (features, *rest)])


def solution(mesh):
    return jax.shard_map(
        body,
        mesh=mesh,
        in_specs=(P(("grp", "frame"), "band", None, None), P(), P(), P(), P(), P(), P()),
        out_specs=P(("grp", "frame"), "band", None, None),
        check_vma=False,
    )
```

```python
import functools

import jax
import jax.numpy as jnp
from jax import lax
from jax.experimental import pallas as pl
from jax.experimental.pallas import tpu as pltpu
from jax.sharding import PartitionSpec as P

LAGS = 2


def rms_silu(values, gain):
    mean = jnp.mean(values * values, axis=-1, keepdims=True)
    half = values * lax.rsqrt(mean + 1e-06) * (0.5 * gain)
    return half + half * jnp.tanh(half)


def dot(left, right):
    return jnp.dot(left, right, preferred_element_type=jnp.float32)


def group_starts(last):
    return sorted({min(max(1, start), last - 1) for start in (1, last - 5, last - 1)})


def kernel(
    features, space_kernel, space_gain, space_bias, time_kernel, time_gain, time_bias,
    out,
    feat, normed, begun, hidden, ntime, earlier, partial, wspace, wtime, vectors,
    feat_sem, weight_sem, halo_recv, time_recv,
):
    frames, rows, cols, channels = features.shape
    half = cols // 2
    split = frames - LAGS + 1
    last = rows - 1
    band, bands = lax.axis_index("band"), lax.axis_size("band")
    frame, frame_parts = lax.axis_index("frame"), lax.axis_size("frame")
    has_up, has_down = band > 0, band < bands - 1
    has_prev, has_next = frame > 0, frame < frame_parts - 1
    neighbours = (
        (has_up, {"band": band - 1}),
        (has_down, {"band": band + 1}),
        (has_prev, {"frame": frame - 1}),
        (has_next, {"frame": frame + 1}),
    )

    barrier = pltpu.get_barrier_semaphore()

    def greet(present, device):
        @pl.when(present)
        def _():
            pl.semaphore_signal(
                barrier, inc=1, device_id=device, device_id_type=pl.DeviceIdType.MESH
            )

    def rows_start(first, count, sem, start=0, size=frames, step=None, width=cols):
        step = step or count
        for f in range(start, start + size):
            for row in range(first, first + count, step):
                for left in range(0, cols, width):
                    columns = pl.ds(left, width)
                    pltpu.make_async_copy(
                        features.at[f, pl.ds(row, step), columns],
                        feat.at[pl.ds(row + 1, step), f, columns],
                        feat_sem.at[sem],
                    ).start()

    def rows_wait(first, count, sem, start=0, size=frames):
        block = feat.at[pl.ds(first + 1, count), pl.ds(start, size)]
        pltpu.make_async_copy(block, block, feat_sem.at[sem]).wait()

    vector_copies = [
        pltpu.make_async_copy(vector, vectors.at[i], weight_sem.at[0])
        for i, vector in enumerate((space_gain, space_bias, time_gain, time_bias))
    ]
    vectors_copy = pltpu.make_async_copy(vectors, vectors, weight_sem.at[0])
    space_copies = [
        pltpu.make_async_copy(
            space_kernel.at[pl.ds(start, count)],
            wspace.at[pl.ds(start, count)],
            weight_sem.at[sem],
        )
        for start, count, sem in ((0, 3, 1), (3, 6, 2))
    ]
    lags_copy = pltpu.make_async_copy(time_kernel, wtime, feat_sem.at[1])
    rows_start(0, 3, 0, 0, split, 1, half)
    for copy in vector_copies:
        copy.start()
    greet(*neighbours[2])
    for copy in space_copies:
        copy.start()
    for i in (0, 1, 3):
        greet(*neighbours[i])
    rows_start(0, 4, 1, split, frames - split)
    rows_start(3, 1, 1, 0, split)

    time_send, halo_send = weight_sem.at[0], weight_sem.at[1]
    groups = group_starts(last)

    def time_copy(source, target, sem):
        return pltpu.make_async_remote_copy(
            source,
            target,
            time_send,
            time_recv.at[sem],
            device_id={"frame": frame + 1},
            device_id_type=pl.DeviceIdType.MESH,
        )

    def row_send(row, sem, start=0, count=LAGS):
        source = ntime.at[row, pl.ds(frames - LAGS + start, count)]
        target = earlier.at[row, pl.ds(start, count)]
        pl.when(has_next)(time_copy(source, target, sem).start)

    def halo_wait(sem):
        for count, present in ((2, has_up & has_down), (1, has_up != has_down)):
            block = feat.at[pl.ds(0, count)]
            pl.when(present)(pltpu.make_async_copy(block, block, sem).wait)

    def time_wait(block, sem):
        pl.when(has_prev)(
            pltpu.make_async_copy(block, block, time_recv.at[sem]).wait
        )

    def vector(i):
        return vectors[i].reshape(1, channels)

    def norm_part(slot, start=0, count=frames):
        size = count * cols
        values = feat[slot, start : start + count]
        result = rms_silu(values.reshape(size, channels).astype(jnp.float32), vector(0))
        column = lax.rem(lax.broadcasted_iota(jnp.int32, (size, channels), 0), cols)
        before = jnp.where(column == 0, 0.0, pltpu.roll(result, 1, 0))
        after = jnp.where(column == cols - 1, 0.0, pltpu.roll(result, size - 1, 0))
        for i, piece in enumerate((before, result, after)):
            normed[
                slot, start : start + count, :, i * channels : (i + 1) * channels
            ] = piece.astype(jnp.bfloat16).reshape(count, cols, channels)

    def taps(block, chosen, start, count):
        total = None
        for i, low, high in chosen:
            columns = slice(low * channels, high * channels)
            parts = [
                normed[row + i, start : start + count, :, columns]
                for row in block
            ]
            parts = [part.reshape(-1, (high - low) * channels) for part in parts]
            left = parts[0] if len(parts) == 1 else jnp.concatenate(parts, 0)
            term = dot(left, wspace[3 * i + low : 3 * i + high].reshape(-1, channels))
            total = term if total is None else total + term
        return total

    def space_store(row, total, start, count):
        shape = (count, cols, channels)
        where = slice(start, start + count)
        centre = feat[row + 1, where].reshape(-1, channels).astype(jnp.float32)
        kept = (centre + total + vector(1)).astype(jnp.bfloat16)
        hidden[row, where] = kept.reshape(shape)
        after = rms_silu(kept.astype(jnp.float32), vector(2))
        ntime[row, where] = after.astype(jnp.bfloat16).reshape(shape)

    def space_part(block, start=0, count=frames, stored=lambda row: None):
        total = taps(block, ((0, 0, 3), (1, 0, 3), (2, 0, 3)), start, count)
        size = count * cols
        for i, row in enumerate(block):
            space_store(row, total[i * size : (i + 1) * size], start, count)
            stored(row)

    def once(step):
        pl.loop(0, 1 + band // bands)(lambda _: step())

    def own_totals(row):
        own = ntime[row]
        totals = [
            dot(own.reshape(-1, channels), wtime[0]).reshape(own.shape)[f]
            for f in range(frames)
        ]
        for lag in range(1, min(LAGS, frames - 1) + 1):
            term = dot(own[: frames - lag].reshape(-1, channels), wtime[lag])
            for f in range(lag, frames):
                totals[f] += term[(f - lag) * cols : (f - lag + 1) * cols]
        return totals

    def finish(row, f, total, left=0, width=cols):
        columns = slice(left, left + width)
        temporal = total.astype(jnp.bfloat16).astype(jnp.float32)
        kept = hidden[row, f, columns].astype(jnp.float32)
        out[f, row, columns] = (kept + temporal + vector(3)).astype(jnp.bfloat16)

    def time_part(row):
        totals = own_totals(row)
        for lag in range(1, LAGS + 1):
            past = earlier[row, LAGS - lag :]
            term = dot(past.reshape(-1, channels), wtime[lag])
            for f in range(lag):
                totals[f] += term[f * cols : (f + 1) * cols]
        for f in range(frames):
            finish(row, f, totals[f])

    def lag_sums(row):
        for f in range(LAGS):
            total = None
            for lag in range(f + 1, LAGS + 1):
                term = dot(ntime[row, frames - lag + f], wtime[lag])
                total = term if total is None else total + term
            partial[f] = total.astype(jnp.bfloat16)

    @pl.when(jnp.logical_not(has_prev))
    def _():
        earlier[...] = jnp.zeros_like(earlier)

    @pl.when(jnp.logical_not(has_up))
    def _():
        feat[0] = jnp.zeros(feat.shape[1:], feat.dtype)

    @pl.when(jnp.logical_not(has_down))
    def _():
        feat[rows + 1] = jnp.zeros(feat.shape[1:], feat.dtype)

    vectors_copy.wait()
    rows_wait(0, 3, 0, 0, split)
    for slot in (1, 2, 3):
        norm_part(slot, 0, split)
    space_copies[0].wait()

    @once
    def _():
        begun[...] = taps((1,), ((0, 0, 3),), 0, split)

    space_copies[1].wait()

    @once
    def _():
        rest = taps((1,), ((1, 0, 3), (2, 0, 3)), 0, split)
        space_store(1, begun[...] + rest, 0, split)

    peers = (
        (band + bands - 1) // bands
        + 1 - (band + 1) // bands
        + (frame + frame_parts - 1) // frame_parts
        + 1 - (frame + 1) // frame_parts
    )
    pl.semaphore_wait(barrier, peers)

    row_send(1, 0, 0, 1)
    to_up = pltpu.make_async_remote_copy(
        features.at[:, 0], feat.at[rows + 1], halo_send, halo_recv.at[0],
        device_id={"band": band - 1}, device_id_type=pl.DeviceIdType.MESH,
    )
    to_down = pltpu.make_async_remote_copy(
        features.at[:, rows - 1], feat.at[0], halo_send, halo_recv.at[0],
        device_id={"band": band + 1}, device_id_type=pl.DeviceIdType.MESH,
    )
    pl.when(has_up)(to_up.start)
    pl.when(has_down)(to_down.start)

    rows_start(4, rows - 4, 0)
    rows_wait(0, 4 * (frames - split) + split, 1, 0, 1)
    lags_copy.start()

    @once
    def _():
        for slot in (1, 2, 3, 4):
            norm_part(slot, split, frames - split)
        space_part(
            (1, 2), split, frames - split, lambda row: row_send(row, 0, 1, LAGS - 1)
        )

    @once
    def _():
        norm_part(4, 0, split)
        space_part((2,), 0, split)

    row_send(2, 0, 0, 1)
    rows_wait(4, rows - 4, 0)

    @pl.loop(3, last)
    def _(row):
        norm_part(row + 2)
        space_part((row,))
        row_send(row, sum((row >= g).astype(jnp.int32) for g in groups[1:]))

    halo_wait(halo_recv.at[0])

    @once
    def _():
        norm_part(0)
        space_part((0,))

    row_send(0, len(groups) - 1)

    @once
    def _():
        norm_part(rows + 1)
        space_part((last,))

    lags_copy.wait()

    @pl.when(has_next)
    def _():
        lag_sums(last)
        for side in range(2):
            columns = pl.ds(side * half, half)
            time_copy(
                partial.at[:, columns],
                earlier.at[last, :, columns],
                len(groups) + side,
            ).start()

    @pl.loop(1, last)
    def _(row):
        for i, start in enumerate(groups):
            count = groups[i + 1] - start if i + 1 < len(groups) else rows - start

            @pl.when(row == start)
            def _():
                time_wait(earlier.at[pl.ds(rows - count, count)], i)

        time_part(row)

    time_part(0)
    totals = own_totals(last)
    for side in range(2):
        columns = slice(side * half, (side + 1) * half)
        time_wait(earlier.at[last, :, pl.ds(side * half, half)], len(groups) + side)
        for f in range(frames):
            total = totals[f][columns]
            if f < LAGS:
                total += earlier[last, f, columns].astype(jnp.float32)
            finish(last, f, total, side * half, half)

    halo_wait(halo_send)

    @pl.when(has_next)
    def _():
        pltpu.make_async_copy(earlier, earlier, time_send).wait()


def body(features, *rest):
    frames, rows, cols, channels = features.shape
    bf16 = jnp.bfloat16
    rest = (rest[0].reshape(-1, channels, channels), *rest[1:])
    return pl.pallas_call(
        kernel,
        out_shape=jax.ShapeDtypeStruct(features.shape, bf16),
        in_specs=[pl.BlockSpec(memory_space=pltpu.HBM)] * 7,
        out_specs=pl.BlockSpec(memory_space=pltpu.VMEM),
        scratch_shapes=[
            pltpu.VMEM((rows + 2, frames, cols, channels), bf16),
            pltpu.VMEM((rows + 2, frames, cols, 3 * channels), bf16),
            pltpu.VMEM(((frames - LAGS + 1) * cols, channels), jnp.float32),
            pltpu.VMEM((rows, frames, cols, channels), bf16),
            pltpu.VMEM((rows, frames, cols, channels), bf16),
            pltpu.VMEM((rows, LAGS, cols, channels), bf16),
            pltpu.VMEM((LAGS, cols, channels), bf16),
            pltpu.VMEM(rest[0].shape, bf16),
            pltpu.VMEM(rest[3].shape, bf16),
            pltpu.VMEM((4, channels), jnp.float32),
            pltpu.SemaphoreType.DMA((2,)),
            pltpu.SemaphoreType.DMA((3,)),
            pltpu.SemaphoreType.DMA((1,)),
            pltpu.SemaphoreType.DMA((len(group_starts(rows - 1)) + 2,)),
        ],
        compiler_params=pltpu.CompilerParams(
            collective_id=0, has_side_effects=True, vmem_limit_bytes=36 * 1024 * 1024
        ),
    )(*[pltpu.with_memory_space_constraint(x, pltpu.HBM) for x in (features, *rest)])


def solution(mesh):
    return jax.shard_map(
        body,
        mesh=mesh,
        in_specs=(P(("grp", "frame"), "band", None, None), P(), P(), P(), P(), P(), P()),
        out_specs=P(("grp", "frame"), "band", None, None),
        check_vma=False,
    )
```

```python
import functools

import jax
import jax.numpy as jnp
from jax import lax
from jax.experimental import pallas as pl
from jax.experimental.pallas import tpu as pltpu
from jax.sharding import PartitionSpec as P

LAGS = 2


def rms_silu(values, gain):
    mean = jnp.mean(values * values, axis=-1, keepdims=True)
    half = values * lax.rsqrt(mean + 1e-06) * (0.5 * gain)
    return half + half * jnp.tanh(half)


def dot(left, right):
    return jnp.dot(left, right, preferred_element_type=jnp.float32)


def group_starts(last):
    return sorted({min(max(1, start), last - 1) for start in (1, last - 5, last - 1)})


def kernel(
    features, space_kernel, space_gain, space_bias, time_kernel, time_gain, time_bias,
    out,
    feat, normed, begun, hidden, ntime, earlier, partial, wspace, wtime, vectors,
    feat_sem, weight_sem, halo_recv, time_recv,
):
    frames, rows, cols, channels = features.shape
    half = cols // 2
    split = frames - LAGS + 1
    last = rows - 1
    band, bands = lax.axis_index("band"), lax.axis_size("band")
    frame, frame_parts = lax.axis_index("frame"), lax.axis_size("frame")
    has_up, has_down = band > 0, band < bands - 1
    has_prev, has_next = frame > 0, frame < frame_parts - 1
    neighbours = (
        (has_up, {"band": band - 1}),
        (has_down, {"band": band + 1}),
        (has_prev, {"frame": frame - 1}),
        (has_next, {"frame": frame + 1}),
    )

    barrier = pltpu.get_barrier_semaphore()

    def greet(present, device):
        @pl.when(present)
        def _():
            pl.semaphore_signal(
                barrier, inc=1, device_id=device, device_id_type=pl.DeviceIdType.MESH
            )

    def rows_start(
        first, count, sem, start=0, size=frames, step=None, width=cols, priority=0
    ):
        step = step or count
        for f in range(start, start + size):
            for row in range(first, first + count, step):
                for left in range(0, cols, width):
                    columns = pl.ds(left, width)
                    pltpu.make_async_copy(
                        features.at[f, pl.ds(row, step), columns],
                        feat.at[pl.ds(row + 1, step), f, columns],
                        feat_sem.at[sem],
                    ).start(priority=priority)

    def rows_wait(first, count, sem, start=0, size=frames):
        block = feat.at[pl.ds(first + 1, count), pl.ds(start, size)]
        pltpu.make_async_copy(block, block, feat_sem.at[sem]).wait()

    vector_copies = [
        pltpu.make_async_copy(vector, vectors.at[i], weight_sem.at[0])
        for i, vector in enumerate((space_gain, space_bias, time_gain, time_bias))
    ]
    vectors_copy = pltpu.make_async_copy(vectors, vectors, weight_sem.at[0])
    space_copies = [
        pltpu.make_async_copy(
            space_kernel.at[pl.ds(start, count)],
            wspace.at[pl.ds(start, count)],
            weight_sem.at[sem],
        )
        for start, count, sem in ((0, 3, 1), (3, 6, 2))
    ]
    lags_copy = pltpu.make_async_copy(time_kernel, wtime, feat_sem.at[2])
    rows_start(0, 3, 0, 0, split, 1, half)
    for copy in vector_copies:
        copy.start()
    greet(*neighbours[2])
    for i, copy in enumerate(space_copies):
        copy.start(priority=i)
    for i in (0, 1, 3):
        greet(*neighbours[i])
    rows_start(0, 4, 1, split, frames - split, priority=1)
    rows_start(3, 1, 2, 0, split, priority=1)

    time_send, up_send, down_send = (weight_sem.at[i] for i in range(3))
    groups = group_starts(last)

    def time_copy(source, target, sem):
        return pltpu.make_async_remote_copy(
            source,
            target,
            time_send,
            time_recv.at[sem],
            device_id={"frame": frame + 1},
            device_id_type=pl.DeviceIdType.MESH,
        )

    def row_send(row, sem, start=0, count=LAGS):
        source = ntime.at[row, pl.ds(frames - LAGS + start, count)]
        target = earlier.at[row, pl.ds(start, count)]
        pl.when(has_next)(time_copy(source, target, sem).start)

    def time_wait(block, sem):
        pl.when(has_prev)(
            pltpu.make_async_copy(block, block, time_recv.at[sem]).wait
        )

    def vector(i):
        return vectors[i].reshape(1, channels)

    def norm_part(slot, start=0, count=frames):
        size = count * cols
        values = feat[slot, start : start + count]
        result = rms_silu(values.reshape(size, channels).astype(jnp.float32), vector(0))
        column = lax.rem(lax.broadcasted_iota(jnp.int32, (size, channels), 0), cols)
        before = jnp.where(column == 0, 0.0, pltpu.roll(result, 1, 0))
        after = jnp.where(column == cols - 1, 0.0, pltpu.roll(result, size - 1, 0))
        for i, piece in enumerate((before, result, after)):
            normed[
                slot, start : start + count, :, i * channels : (i + 1) * channels
            ] = piece.astype(jnp.bfloat16).reshape(count, cols, channels)

    def taps(block, chosen, start, count):
        total = None
        for i, low, high in chosen:
            columns = slice(low * channels, high * channels)
            parts = [
                normed[row + i, start : start + count, :, columns]
                for row in block
            ]
            parts = [part.reshape(-1, (high - low) * channels) for part in parts]
            left = parts[0] if len(parts) == 1 else jnp.concatenate(parts, 0)
            term = dot(left, wspace[3 * i + low : 3 * i + high].reshape(-1, channels))
            total = term if total is None else total + term
        return total

    def space_store(row, total, start, count):
        shape = (count, cols, channels)
        where = slice(start, start + count)
        centre = feat[row + 1, where].reshape(-1, channels).astype(jnp.float32)
        kept = (centre + total + vector(1)).astype(jnp.bfloat16)
        hidden[row, where] = kept.reshape(shape)
        after = rms_silu(kept.astype(jnp.float32), vector(2))
        ntime[row, where] = after.astype(jnp.bfloat16).reshape(shape)

    def space_part(block, start=0, count=frames, stored=lambda row: None):
        total = taps(block, ((0, 0, 3), (1, 0, 3), (2, 0, 3)), start, count)
        size = count * cols
        for i, row in enumerate(block):
            space_store(row, total[i * size : (i + 1) * size], start, count)
            stored(row)

    def once(step):
        pl.loop(0, 1 + band // bands)(lambda _: step())

    def own_totals(row):
        own = ntime[row]
        totals = [
            dot(own.reshape(-1, channels), wtime[0]).reshape(own.shape)[f]
            for f in range(frames)
        ]
        for lag in range(1, min(LAGS, frames - 1) + 1):
            term = dot(own[: frames - lag].reshape(-1, channels), wtime[lag])
            for f in range(lag, frames):
                totals[f] += term[(f - lag) * cols : (f - lag + 1) * cols]
        return totals

    def finish(row, f, total, left=0, width=cols):
        columns = slice(left, left + width)
        temporal = total.astype(jnp.bfloat16).astype(jnp.float32)
        kept = hidden[row, f, columns].astype(jnp.float32)
        out[f, row, columns] = (kept + temporal + vector(3)).astype(jnp.bfloat16)

    def time_part(row):
        totals = own_totals(row)
        for lag in range(1, LAGS + 1):
            past = earlier[row, LAGS - lag :]
            term = dot(past.reshape(-1, channels), wtime[lag])
            for f in range(lag):
                totals[f] += term[f * cols : (f + 1) * cols]
        for f in range(frames):
            finish(row, f, totals[f])

    def lag_sums(row):
        for f in range(LAGS):
            total = None
            for lag in range(f + 1, LAGS + 1):
                term = dot(ntime[row, frames - lag + f], wtime[lag])
                total = term if total is None else total + term
            partial[f] = total.astype(jnp.bfloat16)

    @pl.when(jnp.logical_not(has_prev))
    def _():
        earlier[...] = jnp.zeros_like(earlier)

    @pl.when(jnp.logical_not(has_up))
    def _():
        feat[0] = jnp.zeros(feat.shape[1:], feat.dtype)

    @pl.when(jnp.logical_not(has_down))
    def _():
        feat[rows + 1] = jnp.zeros(feat.shape[1:], feat.dtype)

    vectors_copy.wait()
    rows_wait(0, 3, 0, 0, split)
    for slot in (1, 2, 3):
        norm_part(slot, 0, split)
    space_copies[0].wait()

    @once
    def _():
        begun[...] = taps((1,), ((0, 0, 3),), 0, split)

    space_copies[1].wait()

    @once
    def _():
        rest = taps((1,), ((1, 0, 3), (2, 0, 3)), 0, split)
        space_store(1, begun[...] + rest, 0, split)

    peers = (
        (band + bands - 1) // bands
        + 1 - (band + 1) // bands
        + (frame + frame_parts - 1) // frame_parts
        + 1 - (frame + 1) // frame_parts
    )
    pl.semaphore_wait(barrier, peers)

    row_send(1, 0, 0, 1)
    to_up = pltpu.make_async_remote_copy(
        features.at[:, 0], feat.at[rows + 1], up_send, halo_recv.at[0],
        device_id={"band": band - 1}, device_id_type=pl.DeviceIdType.MESH,
    )
    to_down = pltpu.make_async_remote_copy(
        features.at[:, rows - 1], feat.at[0], down_send, halo_recv.at[1],
        device_id={"band": band + 1}, device_id_type=pl.DeviceIdType.MESH,
    )
    pl.when(has_up)(to_up.start)
    pl.when(has_down)(to_down.start)

    rows_start(4, rows - 4, 0)
    rows_wait(0, 4, 1, split, frames - split)
    rows_wait(3, 1, 2, 0, split)
    lags_copy.start()

    @once
    def _():
        for slot in (1, 2, 3, 4):
            norm_part(slot, split, frames - split)
        space_part(
            (1, 2), split, frames - split, lambda row: row_send(row, 0, 1, LAGS - 1)
        )

    @once
    def _():
        norm_part(4, 0, split)
        space_part((2,), 0, split)

    row_send(2, 0, 0, 1)
    rows_wait(4, rows - 4, 0)

    @pl.loop(3, last)
    def _(row):
        norm_part(row + 2)
        space_part((row,))
        row_send(row, sum((row >= g).astype(jnp.int32) for g in groups[1:]))

    pl.when(has_up)(to_down.wait_recv)
    pl.when(has_down)(to_up.wait_recv)

    @once
    def _():
        norm_part(0)
        space_part((0,))

    row_send(0, len(groups) - 1)

    @once
    def _():
        norm_part(rows + 1)
        space_part((last,))

    lags_copy.wait()

    @pl.when(has_next)
    def _():
        lag_sums(last)
        for side in range(2):
            columns = pl.ds(side * half, half)
            time_copy(
                partial.at[:, columns],
                earlier.at[last, :, columns],
                len(groups) + side,
            ).start()

    @pl.loop(1, last)
    def _(row):
        for i, start in enumerate(groups):
            count = groups[i + 1] - start if i + 1 < len(groups) else rows - start

            @pl.when(row == start)
            def _():
                time_wait(earlier.at[pl.ds(rows - count, count)], i)

        time_part(row)

    time_part(0)
    totals = own_totals(last)
    for side in range(2):
        columns = slice(side * half, (side + 1) * half)
        time_wait(earlier.at[last, :, pl.ds(side * half, half)], len(groups) + side)
        for f in range(frames):
            total = totals[f][columns]
            if f < LAGS:
                total += earlier[last, f, columns].astype(jnp.float32)
            finish(last, f, total, side * half, half)

    pl.when(has_up)(to_up.wait_send)
    pl.when(has_down)(to_down.wait_send)

    @pl.when(has_next)
    def _():
        pltpu.make_async_copy(earlier, earlier, time_send).wait()


def body(features, *rest):
    frames, rows, cols, channels = features.shape
    bf16 = jnp.bfloat16
    rest = (rest[0].reshape(-1, channels, channels), *rest[1:])
    return pl.pallas_call(
        kernel,
        out_shape=jax.ShapeDtypeStruct(features.shape, bf16),
        in_specs=[pl.BlockSpec(memory_space=pltpu.HBM)] * 7,
        out_specs=pl.BlockSpec(memory_space=pltpu.VMEM),
        scratch_shapes=[
            pltpu.VMEM((rows + 2, frames, cols, channels), bf16),
            pltpu.VMEM((rows + 2, frames, cols, 3 * channels), bf16),
            pltpu.VMEM(((frames - LAGS + 1) * cols, channels), jnp.float32),
            pltpu.VMEM((rows, frames, cols, channels), bf16),
            pltpu.VMEM((rows, frames, cols, channels), bf16),
            pltpu.VMEM((rows, LAGS, cols, channels), bf16),
            pltpu.VMEM((LAGS, cols, channels), bf16),
            pltpu.VMEM(rest[0].shape, bf16),
            pltpu.VMEM(rest[3].shape, bf16),
            pltpu.VMEM((4, channels), jnp.float32),
            pltpu.SemaphoreType.DMA((3,)),
            pltpu.SemaphoreType.DMA((3,)),
            pltpu.SemaphoreType.DMA((2,)),
            pltpu.SemaphoreType.DMA((len(group_starts(rows - 1)) + 2,)),
        ],
        compiler_params=pltpu.CompilerParams(
            collective_id=0, has_side_effects=True, vmem_limit_bytes=36 * 1024 * 1024
        ),
    )(*[pltpu.with_memory_space_constraint(x, pltpu.HBM) for x in (features, *rest)])


def solution(mesh):
    return jax.shard_map(
        body,
        mesh=mesh,
        in_specs=(P(("grp", "frame"), "band", None, None), P(), P(), P(), P(), P(), P()),
        out_specs=P(("grp", "frame"), "band", None, None),
        check_vma=False,
    )
```

```python
import functools

import jax
import jax.numpy as jnp
from jax import lax
from jax.experimental import pallas as pl
from jax.experimental.pallas import tpu as pltpu
from jax.sharding import PartitionSpec as P

LAGS = 2


def rms_silu(values, gain):
    mean = jnp.mean(values * values, axis=-1, keepdims=True)
    half = values * lax.rsqrt(mean + 1e-06) * (0.5 * gain)
    return half + half * jnp.tanh(half)


def dot(left, right):
    return jnp.dot(left, right, preferred_element_type=jnp.float32)


def group_starts(last):
    return sorted({min(max(1, start), last - 1) for start in (1, last - 5, last - 1)})


def kernel(
    features, space_kernel, space_gain, space_bias, time_kernel, time_gain, time_bias,
    out,
    feat, normed, begun, hidden, ntime, earlier, partial, wspace, wtime, vectors,
    feat_sem, weight_sem, halo_recv, time_recv,
):
    frames, rows, cols, channels = features.shape
    half = cols // 2
    split = frames - LAGS + 1
    last = rows - 1
    band, bands = lax.axis_index("band"), lax.axis_size("band")
    frame, frame_parts = lax.axis_index("frame"), lax.axis_size("frame")
    has_up, has_down = band > 0, band < bands - 1
    has_prev, has_next = frame > 0, frame < frame_parts - 1
    neighbours = (
        (has_up, {"band": band - 1}),
        (has_down, {"band": band + 1}),
        (has_prev, {"frame": frame - 1}),
        (has_next, {"frame": frame + 1}),
    )

    barrier = pltpu.get_barrier_semaphore()

    def greet(present, device):
        @pl.when(present)
        def _():
            pl.semaphore_signal(
                barrier, inc=1, device_id=device, device_id_type=pl.DeviceIdType.MESH
            )

    def rows_start(
        first, count, sem, start=0, size=frames, step=None, width=cols, priority=0
    ):
        step = step or count
        for f in range(start, start + size):
            for row in range(first, first + count, step):
                for left in range(0, cols, width):
                    columns = pl.ds(left, width)
                    pltpu.make_async_copy(
                        features.at[f, pl.ds(row, step), columns],
                        feat.at[pl.ds(row + 1, step), f, columns],
                        feat_sem.at[sem],
                    ).start(priority=priority)

    def rows_wait(first, count, sem, start=0, size=frames):
        block = feat.at[pl.ds(first + 1, count), pl.ds(start, size)]
        pltpu.make_async_copy(block, block, feat_sem.at[sem]).wait()

    vector_copies = [
        pltpu.make_async_copy(vector, vectors.at[i], weight_sem.at[0])
        for i, vector in enumerate((space_gain, space_bias, time_gain, time_bias))
    ]
    vectors_copy = pltpu.make_async_copy(vectors, vectors, weight_sem.at[0])
    space_copies = [
        pltpu.make_async_copy(
            space_kernel.at[pl.ds(start, count)],
            wspace.at[pl.ds(start, count)],
            weight_sem.at[sem],
        )
        for start, count, sem in ((0, 3, 1), (3, 6, 2))
    ]
    lags_copy = pltpu.make_async_copy(time_kernel, wtime, feat_sem.at[1])
    rows_start(0, 3, 0, 0, split, 1, half)
    for copy in vector_copies:
        copy.start()
    greet(*neighbours[2])
    for i, copy in enumerate(space_copies):
        copy.start(priority=i)
    for i in (0, 1, 3):
        greet(*neighbours[i])
    rows_start(0, 4, 1, split, frames - split, priority=1)
    rows_start(3, 1, 1, 0, split, priority=1)

    time_send, halo_send = weight_sem.at[0], weight_sem.at[1]
    groups = group_starts(last)

    def time_copy(source, target, sem):
        return pltpu.make_async_remote_copy(
            source,
            target,
            time_send,
            time_recv.at[sem],
            device_id={"frame": frame + 1},
            device_id_type=pl.DeviceIdType.MESH,
        )

    def row_send(row, sem, start=0, count=LAGS):
        source = ntime.at[row, pl.ds(frames - LAGS + start, count)]
        target = earlier.at[row, pl.ds(start, count)]
        pl.when(has_next)(time_copy(source, target, sem).start)

    def halo_wait(sem):
        for count, present in ((2, has_up & has_down), (1, has_up != has_down)):
            block = feat.at[pl.ds(0, count)]
            pl.when(present)(pltpu.make_async_copy(block, block, sem).wait)

    def time_wait(block, sem):
        pl.when(has_prev)(
            pltpu.make_async_copy(block, block, time_recv.at[sem]).wait
        )

    def vector(i):
        return vectors[i].reshape(1, channels)

    def norm_part(slot, start=0, count=frames):
        size = count * cols
        values = feat[slot, start : start + count]
        result = rms_silu(values.reshape(size, channels).astype(jnp.float32), vector(0))
        column = lax.rem(lax.broadcasted_iota(jnp.int32, (size, channels), 0), cols)
        before = jnp.where(column == 0, 0.0, pltpu.roll(result, 1, 0))
        after = jnp.where(column == cols - 1, 0.0, pltpu.roll(result, size - 1, 0))
        for i, piece in enumerate((before, result, after)):
            normed[
                slot, start : start + count, :, i * channels : (i + 1) * channels
            ] = piece.astype(jnp.bfloat16).reshape(count, cols, channels)

    def taps(block, chosen, start, count):
        total = None
        for i, low, high in chosen:
            columns = slice(low * channels, high * channels)
            parts = [
                normed[row + i, start : start + count, :, columns]
                for row in block
            ]
            parts = [part.reshape(-1, (high - low) * channels) for part in parts]
            left = parts[0] if len(parts) == 1 else jnp.concatenate(parts, 0)
            term = dot(left, wspace[3 * i + low : 3 * i + high].reshape(-1, channels))
            total = term if total is None else total + term
        return total

    def space_store(row, total, start, count):
        shape = (count, cols, channels)
        where = slice(start, start + count)
        centre = feat[row + 1, where].reshape(-1, channels).astype(jnp.float32)
        kept = (centre + total + vector(1)).astype(jnp.bfloat16)
        hidden[row, where] = kept.reshape(shape)
        after = rms_silu(kept.astype(jnp.float32), vector(2))
        ntime[row, where] = after.astype(jnp.bfloat16).reshape(shape)

    def space_part(block, start=0, count=frames, stored=lambda row: None):
        total = taps(block, ((0, 0, 3), (1, 0, 3), (2, 0, 3)), start, count)
        size = count * cols
        for i, row in enumerate(block):
            space_store(row, total[i * size : (i + 1) * size], start, count)
            stored(row)

    def once(step):
        pl.loop(0, 1 + band // bands)(lambda _: step())

    def own_totals(row):
        own = ntime[row]
        totals = [
            dot(own.reshape(-1, channels), wtime[0]).reshape(own.shape)[f]
            for f in range(frames)
        ]
        for lag in range(1, min(LAGS, frames - 1) + 1):
            term = dot(own[: frames - lag].reshape(-1, channels), wtime[lag])
            for f in range(lag, frames):
                totals[f] += term[(f - lag) * cols : (f - lag + 1) * cols]
        return totals

    def finish(row, f, total, left=0, width=cols):
        columns = slice(left, left + width)
        temporal = total.astype(jnp.bfloat16).astype(jnp.float32)
        kept = hidden[row, f, columns].astype(jnp.float32)
        out[f, row, columns] = (kept + temporal + vector(3)).astype(jnp.bfloat16)

    def time_part(row):
        totals = own_totals(row)
        for lag in range(1, LAGS + 1):
            past = earlier[row, LAGS - lag :]
            term = dot(past.reshape(-1, channels), wtime[lag])
            for f in range(lag):
                totals[f] += term[f * cols : (f + 1) * cols]
        for f in range(frames):
            finish(row, f, totals[f])

    def lag_sums(row):
        for f in range(LAGS):
            total = None
            for lag in range(f + 1, LAGS + 1):
                term = dot(ntime[row, frames - lag + f], wtime[lag])
                total = term if total is None else total + term
            partial[f] = total.astype(jnp.bfloat16)

    @pl.when(jnp.logical_not(has_prev))
    def _():
        earlier[...] = jnp.zeros_like(earlier)

    @pl.when(jnp.logical_not(has_up))
    def _():
        feat[0] = jnp.zeros(feat.shape[1:], feat.dtype)

    @pl.when(jnp.logical_not(has_down))
    def _():
        feat[rows + 1] = jnp.zeros(feat.shape[1:], feat.dtype)

    vectors_copy.wait()
    rows_wait(0, 3, 0, 0, split)
    for slot in (1, 2, 3):
        norm_part(slot, 0, split)
    space_copies[0].wait()

    @once
    def _():
        begun[...] = taps((1,), ((0, 0, 3),), 0, split)

    space_copies[1].wait()

    @once
    def _():
        rest = taps((1,), ((1, 0, 3), (2, 0, 3)), 0, split)
        space_store(1, begun[...] + rest, 0, split)

    peers = (
        (band + bands - 1) // bands
        + 1 - (band + 1) // bands
        + (frame + frame_parts - 1) // frame_parts
        + 1 - (frame + 1) // frame_parts
    )
    pl.semaphore_wait(barrier, peers)

    row_send(1, 0, 0, 1)
    to_up = pltpu.make_async_remote_copy(
        features.at[:, 0], feat.at[rows + 1], halo_send, halo_recv.at[0],
        device_id={"band": band - 1}, device_id_type=pl.DeviceIdType.MESH,
    )
    to_down = pltpu.make_async_remote_copy(
        features.at[:, rows - 1], feat.at[0], halo_send, halo_recv.at[0],
        device_id={"band": band + 1}, device_id_type=pl.DeviceIdType.MESH,
    )
    pl.when(has_up)(to_up.start)
    pl.when(has_down)(to_down.start)

    rows_start(4, rows - 4, 0)
    rows_wait(0, 4 * (frames - split) + split, 1, 0, 1)
    lags_copy.start()

    @once
    def _():
        for slot in (1, 2, 3, 4):
            norm_part(slot, split, frames - split)
        space_part(
            (1, 2), split, frames - split, lambda row: row_send(row, 0, 1, LAGS - 1)
        )

    @once
    def _():
        norm_part(4, 0, split)
        space_part((2,), 0, split)

    row_send(2, 0, 0, 1)
    rows_wait(4, rows - 4, 0)

    @pl.loop(3, last)
    def _(row):
        norm_part(row + 2)
        space_part((row,))
        row_send(row, sum((row >= g).astype(jnp.int32) for g in groups[1:]))

    halo_wait(halo_recv.at[0])

    @once
    def _():
        norm_part(0)
        space_part((0,))

    row_send(0, len(groups) - 1)

    @once
    def _():
        norm_part(rows + 1)
        space_part((last,))

    lags_copy.wait()

    @pl.when(has_next)
    def _():
        lag_sums(last)
        for side in range(2):
            columns = pl.ds(side * half, half)
            time_copy(
                partial.at[:, columns],
                earlier.at[last, :, columns],
                len(groups) + side,
            ).start()

    @pl.loop(1, last)
    def _(row):
        for i, start in enumerate(groups):
            count = groups[i + 1] - start if i + 1 < len(groups) else rows - start

            @pl.when(row == start)
            def _():
                time_wait(earlier.at[pl.ds(rows - count, count)], i)

        time_part(row)

    time_part(0)
    totals = own_totals(last)
    for side in range(2):
        columns = slice(side * half, (side + 1) * half)
        time_wait(earlier.at[last, :, pl.ds(side * half, half)], len(groups) + side)
        for f in range(frames):
            total = totals[f][columns]
            if f < LAGS:
                total += earlier[last, f, columns].astype(jnp.float32)
            finish(last, f, total, side * half, half)

    halo_wait(halo_send)

    @pl.when(has_next)
    def _():
        pltpu.make_async_copy(earlier, earlier, time_send).wait()


def body(features, *rest):
    frames, rows, cols, channels = features.shape
    bf16 = jnp.bfloat16
    rest = (rest[0].reshape(-1, channels, channels), *rest[1:])
    return pl.pallas_call(
        kernel,
        out_shape=jax.ShapeDtypeStruct(features.shape, bf16),
        in_specs=[pl.BlockSpec(memory_space=pltpu.HBM)] * 7,
        out_specs=pl.BlockSpec(memory_space=pltpu.VMEM),
        scratch_shapes=[
            pltpu.VMEM((rows + 2, frames, cols, channels), bf16),
            pltpu.VMEM((rows + 2, frames, cols, 3 * channels), bf16),
            pltpu.VMEM(((frames - LAGS + 1) * cols, channels), jnp.float32),
            pltpu.VMEM((rows, frames, cols, channels), bf16),
            pltpu.VMEM((rows, frames, cols, channels), bf16),
            pltpu.VMEM((rows, LAGS, cols, channels), bf16),
            pltpu.VMEM((LAGS, cols, channels), bf16),
            pltpu.VMEM(rest[0].shape, bf16),
            pltpu.VMEM(rest[3].shape, bf16),
            pltpu.VMEM((4, channels), jnp.float32),
            pltpu.SemaphoreType.DMA((2,)),
            pltpu.SemaphoreType.DMA((3,)),
            pltpu.SemaphoreType.DMA((1,)),
            pltpu.SemaphoreType.DMA((len(group_starts(rows - 1)) + 2,)),
        ],
        compiler_params=pltpu.CompilerParams(
            collective_id=0, has_side_effects=True, vmem_limit_bytes=36 * 1024 * 1024
        ),
    )(*[pltpu.with_memory_space_constraint(x, pltpu.HBM) for x in (features, *rest)])


def solution(mesh):
    return jax.shard_map(
        body,
        mesh=mesh,
        in_specs=(P(("grp", "frame"), "band", None, None), P(), P(), P(), P(), P(), P()),
        out_specs=P(("grp", "frame"), "band", None, None),
        check_vma=False,
    )
```

```python
import functools

import jax
import jax.numpy as jnp
from jax import lax
from jax.experimental import pallas as pl
from jax.experimental.pallas import tpu as pltpu
from jax.sharding import PartitionSpec as P

LAGS = 2


def rms_silu(values, gain):
    mean = jnp.mean(values * values, axis=-1, keepdims=True)
    half = values * lax.rsqrt(mean + 1e-06) * (0.5 * gain)
    return half + half * jnp.tanh(half)


def dot(left, right):
    return jnp.dot(left, right, preferred_element_type=jnp.float32)


def group_starts(last):
    return sorted({min(max(1, start), last - 1) for start in (1, last - 5, last - 1)})


def kernel(
    features, space_kernel, space_gain, space_bias, time_kernel, time_gain, time_bias,
    out,
    feat, normed, begun, hidden, ntime, earlier, partial, wspace, wtime, vectors,
    feat_sem, weight_sem, halo_recv, time_recv,
):
    frames, rows, cols, channels = features.shape
    half = cols // 2
    pieces = ((0, cols - cols // 4), (cols - cols // 4, cols // 4))
    split = frames - LAGS + 1
    last = rows - 1
    band, bands = lax.axis_index("band"), lax.axis_size("band")
    frame, frame_parts = lax.axis_index("frame"), lax.axis_size("frame")
    has_up, has_down = band > 0, band < bands - 1
    has_prev, has_next = frame > 0, frame < frame_parts - 1
    neighbours = (
        (has_up, {"band": band - 1}),
        (has_down, {"band": band + 1}),
        (has_prev, {"frame": frame - 1}),
        (has_next, {"frame": frame + 1}),
    )

    barrier = pltpu.get_barrier_semaphore()

    def greet(present, device):
        @pl.when(present)
        def _():
            pl.semaphore_signal(
                barrier, inc=1, device_id=device, device_id_type=pl.DeviceIdType.MESH
            )

    def rows_start(first, count, sem, start=0, size=frames, step=None, width=cols):
        step = step or count
        for f in range(start, start + size):
            for row in range(first, first + count, step):
                for left in range(0, cols, width):
                    columns = pl.ds(left, width)
                    pltpu.make_async_copy(
                        features.at[f, pl.ds(row, step), columns],
                        feat.at[pl.ds(row + 1, step), f, columns],
                        feat_sem.at[sem],
                    ).start()

    def rows_wait(first, count, sem, start=0, size=frames):
        block = feat.at[pl.ds(first + 1, count), pl.ds(start, size)]
        pltpu.make_async_copy(block, block, feat_sem.at[sem]).wait()

    vector_copies = [
        pltpu.make_async_copy(vector, vectors.at[i], weight_sem.at[0])
        for i, vector in enumerate((space_gain, space_bias, time_gain, time_bias))
    ]
    vectors_copy = pltpu.make_async_copy(vectors, vectors, weight_sem.at[0])
    space_copies = [
        pltpu.make_async_copy(
            space_kernel.at[pl.ds(start, count)],
            wspace.at[pl.ds(start, count)],
            weight_sem.at[sem],
        )
        for start, count, sem in ((0, 3, 1), (3, 6, 2))
    ]
    lags_copy = pltpu.make_async_copy(time_kernel, wtime, feat_sem.at[2])
    rows_start(0, 3, 0, 0, split, 1, half)
    for copy in vector_copies:
        copy.start()
    greet(*neighbours[2])
    for copy in space_copies:
        copy.start()
    for i in (0, 1, 3):
        greet(*neighbours[i])
    rows_start(0, 4, 1, split, frames - split)
    rows_start(3, 1, 2, 0, split)

    time_send, up_send, down_send = (weight_sem.at[i] for i in range(3))
    groups = group_starts(last)

    def time_copy(source, target, sem):
        return pltpu.make_async_remote_copy(
            source,
            target,
            time_send,
            time_recv.at[sem],
            device_id={"frame": frame + 1},
            device_id_type=pl.DeviceIdType.MESH,
        )

    def row_send(row, sem, start=0, count=LAGS):
        source = ntime.at[row, pl.ds(frames - LAGS + start, count)]
        target = earlier.at[row, pl.ds(start, count)]
        pl.when(has_next)(time_copy(source, target, sem).start)

    def time_wait(block, sem):
        pl.when(has_prev)(
            pltpu.make_async_copy(block, block, time_recv.at[sem]).wait
        )

    def vector(i):
        return vectors[i].reshape(1, channels)

    def norm_part(slot, start=0, count=frames):
        size = count * cols
        values = feat[slot, start : start + count]
        result = rms_silu(values.reshape(size, channels).astype(jnp.float32), vector(0))
        column = lax.rem(lax.broadcasted_iota(jnp.int32, (size, channels), 0), cols)
        before = jnp.where(column == 0, 0.0, pltpu.roll(result, 1, 0))
        after = jnp.where(column == cols - 1, 0.0, pltpu.roll(result, size - 1, 0))
        for i, piece in enumerate((before, result, after)):
            normed[
                slot, start : start + count, :, i * channels : (i + 1) * channels
            ] = piece.astype(jnp.bfloat16).reshape(count, cols, channels)

    def taps(block, chosen, start, count):
        total = None
        for i, low, high in chosen:
            columns = slice(low * channels, high * channels)
            parts = [
                normed[row + i, start : start + count, :, columns]
                for row in block
            ]
            parts = [part.reshape(-1, (high - low) * channels) for part in parts]
            left = parts[0] if len(parts) == 1 else jnp.concatenate(parts, 0)
            term = dot(left, wspace[3 * i + low : 3 * i + high].reshape(-1, channels))
            total = term if total is None else total + term
        return total

    def space_store(row, total, start, count):
        shape = (count, cols, channels)
        where = slice(start, start + count)
        centre = feat[row + 1, where].reshape(-1, channels).astype(jnp.float32)
        kept = (centre + total + vector(1)).astype(jnp.bfloat16)
        hidden[row, where] = kept.reshape(shape)
        after = rms_silu(kept.astype(jnp.float32), vector(2))
        ntime[row, where] = after.astype(jnp.bfloat16).reshape(shape)

    def space_part(block, start=0, count=frames, stored=lambda row: None):
        total = taps(block, ((0, 0, 3), (1, 0, 3), (2, 0, 3)), start, count)
        size = count * cols
        for i, row in enumerate(block):
            space_store(row, total[i * size : (i + 1) * size], start, count)
            stored(row)

    def once(step):
        pl.loop(0, 1 + band // bands)(lambda _: step())

    def own_totals(row):
        own = ntime[row]
        totals = [
            dot(own.reshape(-1, channels), wtime[0]).reshape(own.shape)[f]
            for f in range(frames)
        ]
        for lag in range(1, min(LAGS, frames - 1) + 1):
            term = dot(own[: frames - lag].reshape(-1, channels), wtime[lag])
            for f in range(lag, frames):
                totals[f] += term[(f - lag) * cols : (f - lag + 1) * cols]
        return totals

    def finish(row, f, total, left=0, width=cols):
        columns = slice(left, left + width)
        temporal = total.astype(jnp.bfloat16).astype(jnp.float32)
        kept = hidden[row, f, columns].astype(jnp.float32)
        out[f, row, columns] = (kept + temporal + vector(3)).astype(jnp.bfloat16)

    def time_part(row):
        totals = own_totals(row)
        for lag in range(1, LAGS + 1):
            past = earlier[row, LAGS - lag :]
            term = dot(past.reshape(-1, channels), wtime[lag])
            for f in range(lag):
                totals[f] += term[f * cols : (f + 1) * cols]
        for f in range(frames):
            finish(row, f, totals[f])

    def lag_sums(row):
        for f in range(LAGS):
            total = None
            for lag in range(f + 1, LAGS + 1):
                term = dot(ntime[row, frames - lag + f], wtime[lag])
                total = term if total is None else total + term
            partial[f] = total.astype(jnp.bfloat16)

    @pl.when(jnp.logical_not(has_prev))
    def _():
        earlier[...] = jnp.zeros_like(earlier)

    @pl.when(jnp.logical_not(has_up))
    def _():
        feat[0] = jnp.zeros(feat.shape[1:], feat.dtype)

    @pl.when(jnp.logical_not(has_down))
    def _():
        feat[rows + 1] = jnp.zeros(feat.shape[1:], feat.dtype)

    vectors_copy.wait()
    rows_wait(0, 3, 0, 0, split)
    for slot in (1, 2, 3):
        norm_part(slot, 0, split)
    space_copies[0].wait()

    @once
    def _():
        begun[...] = taps((1,), ((0, 0, 3),), 0, split)

    space_copies[1].wait()

    @once
    def _():
        rest = taps((1,), ((1, 0, 3), (2, 0, 3)), 0, split)
        space_store(1, begun[...] + rest, 0, split)

    peers = (
        (band + bands - 1) // bands
        + 1 - (band + 1) // bands
        + (frame + frame_parts - 1) // frame_parts
        + 1 - (frame + 1) // frame_parts
    )
    pl.semaphore_wait(barrier, peers)

    row_send(1, 0, 0, 1)
    to_up = pltpu.make_async_remote_copy(
        features.at[:, 0], feat.at[rows + 1], up_send, halo_recv.at[0],
        device_id={"band": band - 1}, device_id_type=pl.DeviceIdType.MESH,
    )
    to_down = pltpu.make_async_remote_copy(
        features.at[:, rows - 1], feat.at[0], down_send, halo_recv.at[1],
        device_id={"band": band + 1}, device_id_type=pl.DeviceIdType.MESH,
    )
    pl.when(has_up)(to_up.start)
    pl.when(has_down)(to_down.start)

    rows_start(4, rows - 4, 0)
    rows_wait(0, 4, 1, split, frames - split)
    rows_wait(3, 1, 2, 0, split)
    lags_copy.start()

    @once
    def _():
        for slot in (1, 2, 3, 4):
            norm_part(slot, split, frames - split)
        space_part(
            (1, 2), split, frames - split, lambda row: row_send(row, 0, 1, LAGS - 1)
        )

    @once
    def _():
        norm_part(4, 0, split)
        space_part((2,), 0, split)

    row_send(2, 0, 0, 1)
    rows_wait(4, rows - 4, 0)

    @pl.loop(3, last)
    def _(row):
        norm_part(row + 2)
        space_part((row,))
        row_send(row, sum((row >= g).astype(jnp.int32) for g in groups[1:]))

    pl.when(has_up)(to_down.wait_recv)
    pl.when(has_down)(to_up.wait_recv)

    @once
    def _():
        norm_part(0)
        space_part((0,))

    row_send(0, len(groups) - 1)

    @once
    def _():
        norm_part(rows + 1)
        space_part((last,))

    lags_copy.wait()

    @pl.when(has_next)
    def _():
        lag_sums(last)
        for side, (left, width) in enumerate(pieces):
            columns = pl.ds(left, width)
            time_copy(
                partial.at[:, columns],
                earlier.at[last, :, columns],
                len(groups) + side,
            ).start()

    @pl.loop(1, last)
    def _(row):
        for i, start in enumerate(groups):
            count = groups[i + 1] - start if i + 1 < len(groups) else rows - start

            @pl.when(row == start)
            def _():
                time_wait(earlier.at[pl.ds(rows - count, count)], i)

        time_part(row)

    time_part(0)
    totals = own_totals(last)
    for side, (left, width) in enumerate(pieces):
        columns = slice(left, left + width)
        time_wait(earlier.at[last, :, pl.ds(left, width)], len(groups) + side)
        for f in range(frames):
            total = totals[f][columns]
            if f < LAGS:
                total += earlier[last, f, columns].astype(jnp.float32)
            finish(last, f, total, left, width)

    pl.when(has_up)(to_up.wait_send)
    pl.when(has_down)(to_down.wait_send)

    @pl.when(has_next)
    def _():
        pltpu.make_async_copy(earlier, earlier, time_send).wait()


def body(features, *rest):
    frames, rows, cols, channels = features.shape
    bf16 = jnp.bfloat16
    rest = (rest[0].reshape(-1, channels, channels), *rest[1:])
    return pl.pallas_call(
        kernel,
        out_shape=jax.ShapeDtypeStruct(features.shape, bf16),
        in_specs=[pl.BlockSpec(memory_space=pltpu.HBM)] * 7,
        out_specs=pl.BlockSpec(memory_space=pltpu.VMEM),
        scratch_shapes=[
            pltpu.VMEM((rows + 2, frames, cols, channels), bf16),
            pltpu.VMEM((rows + 2, frames, cols, 3 * channels), bf16),
            pltpu.VMEM(((frames - LAGS + 1) * cols, channels), jnp.float32),
            pltpu.VMEM((rows, frames, cols, channels), bf16),
            pltpu.VMEM((rows, frames, cols, channels), bf16),
            pltpu.VMEM((rows, LAGS, cols, channels), bf16),
            pltpu.VMEM((LAGS, cols, channels), bf16),
            pltpu.VMEM(rest[0].shape, bf16),
            pltpu.VMEM(rest[3].shape, bf16),
            pltpu.VMEM((4, channels), jnp.float32),
            pltpu.SemaphoreType.DMA((3,)),
            pltpu.SemaphoreType.DMA((3,)),
            pltpu.SemaphoreType.DMA((2,)),
            pltpu.SemaphoreType.DMA((len(group_starts(rows - 1)) + 2,)),
        ],
        compiler_params=pltpu.CompilerParams(
            collective_id=0, has_side_effects=True, vmem_limit_bytes=36 * 1024 * 1024
        ),
    )(*[pltpu.with_memory_space_constraint(x, pltpu.HBM) for x in (features, *rest)])


def solution(mesh):
    return jax.shard_map(
        body,
        mesh=mesh,
        in_specs=(P(("grp", "frame"), "band", None, None), P(), P(), P(), P(), P(), P()),
        out_specs=P(("grp", "frame"), "band", None, None),
        check_vma=False,
    )
```

```python
import functools

import jax
import jax.numpy as jnp
from jax import lax
from jax.experimental import pallas as pl
from jax.experimental.pallas import tpu as pltpu
from jax.sharding import PartitionSpec as P

LAGS = 2


def rms_silu(values, gain):
    mean = jnp.mean(values * values, axis=-1, keepdims=True)
    half = values * lax.rsqrt(mean + 1e-06) * (0.5 * gain)
    return half + half * jnp.tanh(half)


def dot(left, right):
    return jnp.dot(left, right, preferred_element_type=jnp.float32)


def group_starts(last):
    return sorted({min(max(1, start), last - 1) for start in (1, last - 5, last - 1)})


def kernel(
    features, space_kernel, space_gain, space_bias, time_kernel, time_gain, time_bias,
    out,
    feat, normed, begun, hidden, ntime, earlier, partial, wspace, wtime, vectors,
    feat_sem, weight_sem, halo_recv, time_recv,
):
    frames, rows, cols, channels = features.shape
    half = cols // 2
    pieces = ((0, cols - cols // 4), (cols - cols // 4, cols // 4))
    split = frames - LAGS + 1
    last = rows - 1
    band, bands = lax.axis_index("band"), lax.axis_size("band")
    frame, frame_parts = lax.axis_index("frame"), lax.axis_size("frame")
    has_up, has_down = band > 0, band < bands - 1
    has_prev, has_next = frame > 0, frame < frame_parts - 1
    neighbours = (
        (has_up, {"band": band - 1}),
        (has_down, {"band": band + 1}),
        (has_prev, {"frame": frame - 1}),
        (has_next, {"frame": frame + 1}),
    )

    barrier = pltpu.get_barrier_semaphore()

    def greet(present, device):
        @pl.when(present)
        def _():
            pl.semaphore_signal(
                barrier, inc=1, device_id=device, device_id_type=pl.DeviceIdType.MESH
            )

    def rows_start(
        first, count, sem, start=0, size=frames, step=None, width=cols, priority=0
    ):
        step = step or count
        for f in range(start, start + size):
            for row in range(first, first + count, step):
                for left in range(0, cols, width):
                    columns = pl.ds(left, width)
                    pltpu.make_async_copy(
                        features.at[f, pl.ds(row, step), columns],
                        feat.at[pl.ds(row + 1, step), f, columns],
                        feat_sem.at[sem],
                    ).start(priority=priority)

    def rows_wait(first, count, sem, start=0, size=frames):
        block = feat.at[pl.ds(first + 1, count), pl.ds(start, size)]
        pltpu.make_async_copy(block, block, feat_sem.at[sem]).wait()

    vector_copies = [
        pltpu.make_async_copy(vector, vectors.at[i], weight_sem.at[0])
        for i, vector in enumerate((space_gain, space_bias, time_gain, time_bias))
    ]
    vectors_copy = pltpu.make_async_copy(vectors, vectors, weight_sem.at[0])
    space_copies = [
        pltpu.make_async_copy(
            space_kernel.at[pl.ds(start, count)],
            wspace.at[pl.ds(start, count)],
            weight_sem.at[sem],
        )
        for start, count, sem in ((0, 3, 1), (3, 6, 2))
    ]
    lags_copy = pltpu.make_async_copy(time_kernel, wtime, feat_sem.at[1])
    rows_start(0, 3, 0, 0, split, 1, half)
    for copy in vector_copies:
        copy.start()
    greet(*neighbours[2])
    for i, copy in enumerate(space_copies):
        copy.start(priority=i)
    for i in (0, 1, 3):
        greet(*neighbours[i])
    rows_start(0, 4, 1, split, frames - split, priority=1)
    rows_start(3, 1, 1, 0, split, priority=1)

    time_send, halo_send = weight_sem.at[0], weight_sem.at[1]
    groups = group_starts(last)

    def time_copy(source, target, sem):
        return pltpu.make_async_remote_copy(
            source,
            target,
            time_send,
            time_recv.at[sem],
            device_id={"frame": frame + 1},
            device_id_type=pl.DeviceIdType.MESH,
        )

    def row_send(row, sem, start=0, count=LAGS):
        source = ntime.at[row, pl.ds(frames - LAGS + start, count)]
        target = earlier.at[row, pl.ds(start, count)]
        pl.when(has_next)(time_copy(source, target, sem).start)

    def halo_wait(sem):
        for count, present in ((2, has_up & has_down), (1, has_up != has_down)):
            block = feat.at[pl.ds(0, count)]
            pl.when(present)(pltpu.make_async_copy(block, block, sem).wait)

    def time_wait(block, sem):
        pl.when(has_prev)(
            pltpu.make_async_copy(block, block, time_recv.at[sem]).wait
        )

    def vector(i):
        return vectors[i].reshape(1, channels)

    def norm_part(slot, start=0, count=frames):
        size = count * cols
        values = feat[slot, start : start + count]
        result = rms_silu(values.reshape(size, channels).astype(jnp.float32), vector(0))
        column = lax.rem(lax.broadcasted_iota(jnp.int32, (size, channels), 0), cols)
        before = jnp.where(column == 0, 0.0, pltpu.roll(result, 1, 0))
        after = jnp.where(column == cols - 1, 0.0, pltpu.roll(result, size - 1, 0))
        for i, piece in enumerate((before, result, after)):
            normed[
                slot, start : start + count, :, i * channels : (i + 1) * channels
            ] = piece.astype(jnp.bfloat16).reshape(count, cols, channels)

    def taps(block, chosen, start, count):
        total = None
        for i, low, high in chosen:
            columns = slice(low * channels, high * channels)
            parts = [
                normed[row + i, start : start + count, :, columns]
                for row in block
            ]
            parts = [part.reshape(-1, (high - low) * channels) for part in parts]
            left = parts[0] if len(parts) == 1 else jnp.concatenate(parts, 0)
            term = dot(left, wspace[3 * i + low : 3 * i + high].reshape(-1, channels))
            total = term if total is None else total + term
        return total

    def space_store(row, total, start, count):
        shape = (count, cols, channels)
        where = slice(start, start + count)
        centre = feat[row + 1, where].reshape(-1, channels).astype(jnp.float32)
        kept = (centre + total + vector(1)).astype(jnp.bfloat16)
        hidden[row, where] = kept.reshape(shape)
        after = rms_silu(kept.astype(jnp.float32), vector(2))
        ntime[row, where] = after.astype(jnp.bfloat16).reshape(shape)

    def space_part(block, start=0, count=frames, stored=lambda row: None):
        total = taps(block, ((0, 0, 3), (1, 0, 3), (2, 0, 3)), start, count)
        size = count * cols
        for i, row in enumerate(block):
            space_store(row, total[i * size : (i + 1) * size], start, count)
            stored(row)

    def once(step):
        pl.loop(0, 1 + band // bands)(lambda _: step())

    def own_totals(row):
        own = ntime[row]
        totals = [
            dot(own.reshape(-1, channels), wtime[0]).reshape(own.shape)[f]
            for f in range(frames)
        ]
        for lag in range(1, min(LAGS, frames - 1) + 1):
            term = dot(own[: frames - lag].reshape(-1, channels), wtime[lag])
            for f in range(lag, frames):
                totals[f] += term[(f - lag) * cols : (f - lag + 1) * cols]
        return totals

    def finish(row, f, total, left=0, width=cols):
        columns = slice(left, left + width)
        temporal = total.astype(jnp.bfloat16).astype(jnp.float32)
        kept = hidden[row, f, columns].astype(jnp.float32)
        out[f, row, columns] = (kept + temporal + vector(3)).astype(jnp.bfloat16)

    def time_part(row):
        totals = own_totals(row)
        for lag in range(1, LAGS + 1):
            past = earlier[row, LAGS - lag :]
            term = dot(past.reshape(-1, channels), wtime[lag])
            for f in range(lag):
                totals[f] += term[f * cols : (f + 1) * cols]
        for f in range(frames):
            finish(row, f, totals[f])

    def lag_sums(row):
        for f in range(LAGS):
            total = None
            for lag in range(f + 1, LAGS + 1):
                term = dot(ntime[row, frames - lag + f], wtime[lag])
                total = term if total is None else total + term
            partial[f] = total.astype(jnp.bfloat16)

    @pl.when(jnp.logical_not(has_prev))
    def _():
        earlier[...] = jnp.zeros_like(earlier)

    @pl.when(jnp.logical_not(has_up))
    def _():
        feat[0] = jnp.zeros(feat.shape[1:], feat.dtype)

    @pl.when(jnp.logical_not(has_down))
    def _():
        feat[rows + 1] = jnp.zeros(feat.shape[1:], feat.dtype)

    vectors_copy.wait()
    rows_wait(0, 3, 0, 0, split)
    for slot in (1, 2, 3):
        norm_part(slot, 0, split)
    space_copies[0].wait()

    @once
    def _():
        begun[...] = taps((1,), ((0, 0, 3),), 0, split)

    space_copies[1].wait()

    @once
    def _():
        rest = taps((1,), ((1, 0, 3), (2, 0, 3)), 0, split)
        space_store(1, begun[...] + rest, 0, split)

    peers = (
        (band + bands - 1) // bands
        + 1 - (band + 1) // bands
        + (frame + frame_parts - 1) // frame_parts
        + 1 - (frame + 1) // frame_parts
    )
    pl.semaphore_wait(barrier, peers)

    row_send(1, 0, 0, 1)
    to_up = pltpu.make_async_remote_copy(
        features.at[:, 0], feat.at[rows + 1], halo_send, halo_recv.at[0],
        device_id={"band": band - 1}, device_id_type=pl.DeviceIdType.MESH,
    )
    to_down = pltpu.make_async_remote_copy(
        features.at[:, rows - 1], feat.at[0], halo_send, halo_recv.at[0],
        device_id={"band": band + 1}, device_id_type=pl.DeviceIdType.MESH,
    )
    pl.when(has_up)(to_up.start)
    pl.when(has_down)(to_down.start)

    rows_start(4, rows - 4, 0)
    rows_wait(0, 4 * (frames - split) + split, 1, 0, 1)
    lags_copy.start()

    @once
    def _():
        for slot in (1, 2, 3, 4):
            norm_part(slot, split, frames - split)
        space_part(
            (1, 2), split, frames - split, lambda row: row_send(row, 0, 1, LAGS - 1)
        )

    @once
    def _():
        norm_part(4, 0, split)
        space_part((2,), 0, split)

    row_send(2, 0, 0, 1)
    rows_wait(4, rows - 4, 0)

    @pl.loop(3, last)
    def _(row):
        norm_part(row + 2)
        space_part((row,))
        row_send(row, sum((row >= g).astype(jnp.int32) for g in groups[1:]))

    halo_wait(halo_recv.at[0])

    @once
    def _():
        norm_part(0)
        space_part((0,))

    row_send(0, len(groups) - 1)

    @once
    def _():
        norm_part(rows + 1)
        space_part((last,))

    lags_copy.wait()

    @pl.when(has_next)
    def _():
        lag_sums(last)
        for side, (left, width) in enumerate(pieces):
            columns = pl.ds(left, width)
            time_copy(
                partial.at[:, columns],
                earlier.at[last, :, columns],
                len(groups) + side,
            ).start()

    @pl.loop(1, last)
    def _(row):
        for i, start in enumerate(groups):
            count = groups[i + 1] - start if i + 1 < len(groups) else rows - start

            @pl.when(row == start)
            def _():
                time_wait(earlier.at[pl.ds(rows - count, count)], i)

        time_part(row)

    time_part(0)
    totals = own_totals(last)
    for side, (left, width) in enumerate(pieces):
        columns = slice(left, left + width)
        time_wait(earlier.at[last, :, pl.ds(left, width)], len(groups) + side)
        for f in range(frames):
            total = totals[f][columns]
            if f < LAGS:
                total += earlier[last, f, columns].astype(jnp.float32)
            finish(last, f, total, left, width)

    halo_wait(halo_send)

    @pl.when(has_next)
    def _():
        pltpu.make_async_copy(earlier, earlier, time_send).wait()


def body(features, *rest):
    frames, rows, cols, channels = features.shape
    bf16 = jnp.bfloat16
    rest = (rest[0].reshape(-1, channels, channels), *rest[1:])
    return pl.pallas_call(
        kernel,
        out_shape=jax.ShapeDtypeStruct(features.shape, bf16),
        in_specs=[pl.BlockSpec(memory_space=pltpu.HBM)] * 7,
        out_specs=pl.BlockSpec(memory_space=pltpu.VMEM),
        scratch_shapes=[
            pltpu.VMEM((rows + 2, frames, cols, channels), bf16),
            pltpu.VMEM((rows + 2, frames, cols, 3 * channels), bf16),
            pltpu.VMEM(((frames - LAGS + 1) * cols, channels), jnp.float32),
            pltpu.VMEM((rows, frames, cols, channels), bf16),
            pltpu.VMEM((rows, frames, cols, channels), bf16),
            pltpu.VMEM((rows, LAGS, cols, channels), bf16),
            pltpu.VMEM((LAGS, cols, channels), bf16),
            pltpu.VMEM(rest[0].shape, bf16),
            pltpu.VMEM(rest[3].shape, bf16),
            pltpu.VMEM((4, channels), jnp.float32),
            pltpu.SemaphoreType.DMA((2,)),
            pltpu.SemaphoreType.DMA((3,)),
            pltpu.SemaphoreType.DMA((1,)),
            pltpu.SemaphoreType.DMA((len(group_starts(rows - 1)) + 2,)),
        ],
        compiler_params=pltpu.CompilerParams(
            collective_id=0, has_side_effects=True, vmem_limit_bytes=36 * 1024 * 1024
        ),
    )(*[pltpu.with_memory_space_constraint(x, pltpu.HBM) for x in (features, *rest)])


def solution(mesh):
    return jax.shard_map(
        body,
        mesh=mesh,
        in_specs=(P(("grp", "frame"), "band", None, None), P(), P(), P(), P(), P(), P()),
        out_specs=P(("grp", "frame"), "band", None, None),
        check_vma=False,
    )
```
